32 devices in a mesh: group: 2 (over y), tm: 4 (over z), tensor: 2 (over x), dp: 2 (over core).
Axes of the slice: x: 2, y: 2, z: 4, core: 2. Of those that a mesh axis runs over, the one named last changes fastest.
Arguments:
- frames_in: bfloat16 [4, 3072, 1024], P(('group', 'dp'), 'tm', 'tensor'), parts along dimension 0, may hold values from -6 to 6
- in_proj: bfloat16 [2, 1024, 1024], P(None, None, 'tensor'), may hold values from -0.1875 to 0.1875
- log_rates: float32 [8, 8], P(None, 'tensor'), as said below
- angles: float32 [8, 8], P(None, 'tensor'), may hold values from -3.140625 to 3.140625
- residues: float32 [2, 8, 1024], P(None, None, 'tensor'), may hold values from -3 to 3
- skip_gain: float32 [1024], P('tensor'), may hold values from -3 to 3
- lengths: int32 [4, 4], P(('group', 'dp')), parts along dimension 0, may hold values from 1 to 1536, 3072 in all within a row
- grad_out: bfloat16 [4, 3072, 1024], P(('group', 'dp'), 'tm', 'tensor'), parts along dimension 0, may hold values from -6 to 6
Outputs:
- mixed: bfloat16 [4, 3072, 1024], P(('group', 'dp'), 'tm', 'tensor'), parts along dimension 0
- input_grad: bfloat16 [4, 3072, 1024], P(('group', 'dp'), 'tm', 'tensor'), parts along dimension 0
- proj_grad: float32 [4, 1024, 1024], P('group', None, 'tensor'), parts along dimension 0
- residue_grad: float32 [4, 8, 1024], P('group', None, 'tensor'), parts along dimension 0
- skip_grad: float32 [2048], P(('group', 'tensor')), parts along dimension 0
The draws below stay inside these ranges and needn't reach their ends.
There are 2 independent parts, one for each index of `group`. The reference program is written for one: setup_inputs(seed, part) draws one part's arguments, and reference() takes and returns one part's arrays. A program takes and returns all parts, laid end to end along the dimension named above; an argument that names none is the same for every part. Nothing has to cross between parts.
Inputs may be any that keep to these rules, and one draw needn't show every extreme that they name: Each clip has at least one frame; the lengths of a stream sum to 3072. `log_rates`: each entry lies between the logarithms of 0.1 / 3072 and 0.08.
All inputs are finite; a program needn't handle non-finite values.
Results may differ from the reference program's by a relative error of at most 0.0058.
Values may be sent and summed in bfloat16 or wider, within the bound.
A program may use at most 128 MiB of HBM per device.

```python
import math
import jax
import jax.numpy as jnp
import numpy as np
from jax import lax

HEADS = 8
HEAD_DIM = 128
WIDTH = 1024
MODES = 8
BLOCK_LEN = 128
CLIPS = 4
FRAMES = 3072
STREAMS = 2


def draw_log_rates(key, part):
    key_mask, key_slow, key_fast = jax.random.split(jax.random.fold_in(key, 7), 3)
    slow_share = 0.5
    slow_rates = jax.random.uniform(key_slow, (MODES, HEADS), jnp.float32, math.log(0.1 / FRAMES), math.log(1.0 / FRAMES))
    fast_rates = jax.random.uniform(key_fast, (MODES, HEADS), jnp.float32, math.log(0.03), math.log(0.08))
    picker = jax.random.uniform(key_mask, (MODES, HEADS), jnp.float32)
    return jnp.where(picker < slow_share, slow_rates, fast_rates)


def block_scale(rng, shape, pieces, smallest, largest):
    def one(dim, blocks):
        heights = jax.random.uniform(jax.random.fold_in(jax.random.fold_in(rng, 6), dim), (blocks,), jnp.float32, smallest / len(pieces), largest / len(pieces))
        return jnp.repeat(jnp.exp(heights), shape[dim] // blocks).reshape((-1,) + (1,) * (len(shape) - dim - 1))

    level = one(*pieces[0])
    for cut in pieces[1:]:
        level = level * one(*cut)
    return level


def split_up(number_of, total, limit, lean):
    loads = [(1 << 20) // math.isqrt(rank ** lean) + 1 for rank in range(2, number_of + 1)]
    rest, given = total - limit - (number_of - 1), [1] * (number_of - 1)
    while rest > 0:
        candidates = [i for i in range(number_of - 1) if given[i] < limit]
        mass, budget = sum([loads[i] for i in candidates]), rest
        for i in candidates:
            extra = min(limit - given[i], max(1, budget * loads[i] // mass), rest)
            given[i] = given[i] + extra
            rest = rest - extra
    return np.array([limit] + given)


def uneven(stream_key, count, total, most, slope):
    if count == 2:
        one = jax.random.randint(stream_key, (), max(1, total - most), min(most, total - 1) + 1)
        return jnp.stack([one, total - one])
    tallies = jnp.asarray(split_up(count, total, most, slope), jnp.int32)
    twos = (count - 1) // 2
    source_of, taker = tallies[1:1 + 2 * twos:2], tallies[2:2 + 2 * twos:2]
    slack = jnp.minimum(source_of - 1, most - taker)
    shifted = jax.random.randint(jax.random.fold_in(stream_key, 1), (twos,), 0, 1 << 20) % (slack + 1)
    tallies = tallies.at[1:1 + 2 * twos:2].set(source_of - shifted).at[2:2 + 2 * twos:2].set(taker + shifted)
    return tallies[jax.random.permutation(jax.random.fold_in(stream_key, 2), count)]


def noise(stream_key, dims, width, bound, cuts=(), kind=jnp.bfloat16):
    values = width * jax.random.normal(stream_key, dims, jnp.float32)
    if cuts:
        values = values * block_scale(stream_key, dims, cuts, -0.22, 0.18)
    return jnp.clip(values, -bound, bound).astype(kind)


def setup_inputs(seed: int = 0, part: int = 0) -> dict:
    keys = jax.random.split(jax.random.key(seed), 9)
    part_splits = jax.random.split(jax.random.fold_in(keys[8], part), 9)
    frames_in = noise(part_splits[0], (STREAMS, FRAMES, WIDTH), 1.0, 6.0, ((0, 2), (1, 4), (2, 2)))
    in_proj = noise(keys[1], (2, WIDTH, WIDTH), WIDTH ** -0.5, 0.1875, ((2, 2),))
    log_rates = draw_log_rates(jax.random.fold_in(keys[8], 71), part)
    angles = jnp.clip(jax.random.uniform(keys[3], (MODES, HEADS), jnp.float32, -3.140625, 3.140625), -3.140625, 3.140625)
    residues = noise(keys[4], (2, MODES, WIDTH), 0.5, 3.0, ((2, 2),), jnp.float32)
    skip_gain = noise(keys[5], (WIDTH,), 0.5, 3.0, ((0, 2),), jnp.float32)
    lengths = jax.vmap(lambda own: uneven(own, CLIPS, FRAMES, FRAMES // 2, 2))(jax.random.split(part_splits[6], STREAMS)).reshape((STREAMS, CLIPS)).astype(jnp.int32)
    grad_out = noise(part_splits[7], (STREAMS, FRAMES, WIDTH), 1.0, 6.0, ((0, 2), (1, 4), (2, 2)))
    return {"frames_in": frames_in, "in_proj": in_proj, "log_rates": log_rates, "angles": angles, "residues": residues, "skip_gain": skip_gain, "lengths": lengths, "grad_out": grad_out}


def pole_terms(log_rates, angles):
    decay_rate = jnp.exp(log_rates)
    magnitude = jnp.exp(-decay_rate)
    weight = jnp.sqrt(-jnp.expm1(-2.0 * decay_rate))
    return (magnitude * jnp.cos(angles), magnitude * jnp.sin(angles), weight)

def long_conv(signal, coeffs, skip_vec, pole_real, pole_imag, weight, keep_mask):
    streams, frames, features = signal.shape
    coefficient_real = coeffs[0].reshape(MODES, HEADS, HEAD_DIM) * weight[:, :, None]
    coefficient_imaginary = coeffs[1].reshape(MODES, HEADS, HEAD_DIM) * weight[:, :, None]
    skip_row = skip_vec.reshape(HEADS, HEAD_DIM)
    blocks = frames // BLOCK_LEN
    inputs = signal.reshape(streams, blocks, BLOCK_LEN, HEADS, HEAD_DIM).transpose(1, 2, 0, 3, 4)
    resets = keep_mask.reshape(streams, blocks, BLOCK_LEN).transpose(1, 2, 0)
    real_part = pole_real[None, :, :, None]
    imag_part = pole_imag[None, :, :, None]

    def frame_step(carried, element):
        state_re, state_im = carried
        current, kept = element
        factor = kept[:, None, None, None]
        next_re = factor * (real_part * state_re - imag_part * state_im) + current[:, None]
        next_im = factor * (real_part * state_im + imag_part * state_re)
        output = skip_row * current + lax.optimization_barrier(jnp.sum(coefficient_real * next_re - coefficient_imaginary * next_im, axis=1))
        return ((next_re, next_im), output)

    def block_step(carried, element):
        return lax.scan(frame_step, carried, element)
    initial = jnp.zeros((streams, MODES, HEADS, HEAD_DIM), jnp.float32)
    _, outputs = lax.scan(jax.checkpoint(block_step), (initial, initial), (inputs, resets))
    return outputs.transpose(2, 0, 1, 3, 4).reshape(streams, frames, features)

def reference(frames_in, in_proj, log_rates, angles, residues, skip_gain, lengths, grad_out):
    inputs32 = frames_in.astype(jnp.float32)
    weights32 = in_proj.astype(jnp.float32)
    query_rows = jnp.einsum('bfd,dc->bfc', inputs32, weights32[0]).astype(jnp.bfloat16)
    signal = jnp.einsum('bfd,dc->bfc', inputs32, weights32[1]).astype(jnp.bfloat16)
    pole_real, pole_imag, weight = pole_terms(log_rates, angles)
    clip_start = (jnp.cumsum(lengths, axis=1) - lengths).astype(jnp.int32)
    frame_ids = jnp.arange(FRAMES, dtype=jnp.int32)
    is_start = jnp.any(frame_ids[None, :, None] == clip_start[:, None, :], axis=2)
    keep_mask = jnp.where(is_start, 0.0, 1.0).astype(jnp.float32)

    def convolve(signal32, coeffs, skip_vec):
        return long_conv(signal32, coeffs, skip_vec, pole_real, pole_imag, weight, keep_mask)
    long_out, pullback = jax.vjp(convolve, signal.astype(jnp.float32), residues, skip_gain)
    query32 = query_rows.astype(jnp.float32)
    upstream = grad_out.astype(jnp.float32)
    mixed = (query32 * long_out).astype(jnp.bfloat16)
    grad_long = upstream * query32
    grad_query = (upstream * long_out).astype(jnp.bfloat16)
    grad_signal, grad_coeffs, grad_skip = pullback(grad_long)
    grad_value = grad_signal.astype(jnp.bfloat16)
    query_grad32 = grad_query.astype(jnp.float32)
    value_grad32 = grad_value.astype(jnp.float32)
    input_grad = (jnp.einsum('bfc,dc->bfd', query_grad32, weights32[0]) + jnp.einsum('bfc,dc->bfd', value_grad32, weights32[1])).astype(jnp.bfloat16)
    norm_scale = 1.0 / math.sqrt(FRAMES * STREAMS)
    proj_grad = jnp.stack([jnp.einsum('bfd,bfc->dc', inputs32, query_grad32), jnp.einsum('bfd,bfc->dc', inputs32, value_grad32)]) * norm_scale
    return (mixed, input_grad, proj_grad, grad_coeffs * norm_scale, grad_skip * norm_scale)
```

```python
import functools
import math

import jax
import jax.numpy as jnp
from jax import lax
from jax.experimental import pallas as pl
from jax.experimental.pallas import tpu as pltpu
from jax.sharding import PartitionSpec as P

BLOCK_LEN = 128
F32 = jnp.float32
BF16 = jnp.bfloat16


def dot(a, b):
    return jnp.dot(a, b, preferred_element_type=F32)


def segment_of(starts_ref, clips, frame):
    total = jnp.where(frame >= starts_ref[1], 1, 0)
    for k in range(1, clips):
        total = total + jnp.where(frame >= starts_ref[1 + k], 1, 0)
    return total


def project_kernel(clips, modes, starts_ref, feat_ref, proj_ref, up_ref, table_ref, q_ref, x_ref, ends_ref):
    rows, width = q_ref.shape
    first = starts_ref[0]
    lane = lax.broadcasted_iota(jnp.int32, (1, rows), 1) + first
    seg = segment_of(starts_ref, clips, lane)
    at_end = jnp.where(seg == segment_of(starts_ref, clips, first + rows - 1), 1.0, 0.0)
    at_start = jnp.where(seg == segment_of(starts_ref, clips, first), 1.0, 0.0)
    query = dot(feat_ref[...], proj_ref[0]).astype(BF16)
    q_ref[...] = query
    signal = dot(feat_ref[...], proj_ref[1]).astype(BF16)
    x_ref[...] = signal
    grad = (query.astype(F32) * up_ref[...].astype(F32)).astype(BF16)
    for h in range(width // 128):
        cols = slice(h * 128, h * 128 + 128)
        fwd = (table_ref[h, : 2 * modes, :] * at_end).astype(BF16)
        bwd = (table_ref[h, 2 * modes :, :] * at_start).astype(BF16)
        ends_ref[h, : 2 * modes, :] = dot(fwd, signal[:, cols])
        ends_ref[h, 2 * modes :, :] = dot(bwd, grad[:, cols])


def conv_kernel(
    clips, modes, starts_ref, cols_ref, rows_ref, w_ref, carry_ref, q_ref, x_ref, up_ref,
    mixed_ref, stack_ref, sums_ref, kf, kb, tx,
):
    rows = q_ref.shape[0]
    blocks = rows // BLOCK_LEN
    M = modes
    first = starts_ref[0]
    i0 = lax.broadcasted_iota(jnp.int32, (BLOCK_LEN, BLOCK_LEN), 0)
    i1 = lax.broadcasted_iota(jnp.int32, (BLOCK_LEN, BLOCK_LEN), 1)
    for m in range(M):
        re, im = m, M + m
        er, ei = cols_ref[0, :, re : re + 1], cols_ref[0, :, im : im + 1]
        fr = rows_ref[0, 2 * M + re : 2 * M + re + 1, :]
        fi = rows_ref[0, 2 * M + im : 2 * M + im + 1, :]
        kf[:, re * 128 : re * 128 + 128] = jnp.where(i0 >= i1, er * fr - ei * fi, 0.0).astype(BF16)
        kf[:, im * 128 : im * 128 + 128] = jnp.where(i0 >= i1, -(er * fi + ei * fr), 0.0).astype(BF16)
        fr, fi = cols_ref[0, :, 2 * M + re : 2 * M + re + 1], cols_ref[0, :, 2 * M + im : 2 * M + im + 1]
        er, ei = rows_ref[0, re : re + 1, :], rows_ref[0, im : im + 1, :]
        kb[re * 128 : re * 128 + 128, :] = jnp.where(i1 >= i0, er * fr - ei * fi, 0.0).astype(BF16)
        kb[im * 128 : im * 128 + 128, :] = jnp.where(i1 >= i0, -(er * fi + ei * fr), 0.0).astype(BF16)

    w = w_ref[0, : 2 * M, :]
    wr, wi = w[:M], w[M:]
    skip = w_ref[0, 2 * M : 2 * M + 1, :]
    pr = rows_ref[0, 6 * M : 7 * M, :]
    pi = rows_ref[0, 7 * M : 8 * M, :]
    col_p = cols_ref[0, :, : 2 * M].astype(BF16)
    col_h = cols_ref[0, :, 4 * M : 6 * M].astype(BF16)

    def flag(cond):
        return jnp.where(cond, 1.0, 0.0).astype(F32)

    def weigh(sr, si):
        return jnp.concatenate([wr * sr - wi * si, -(wr * si + wi * sr)], axis=0).astype(BF16)

    def masks(b):
        begin = first + b * BLOCK_LEN
        seg0 = segment_of(starts_ref, clips, i0 + begin)
        seg1 = segment_of(starts_ref, clips, i1 + begin)
        prior = segment_of(starts_ref, clips, begin - 1)
        head = segment_of(starts_ref, clips, begin)
        last = segment_of(starts_ref, clips, begin + BLOCK_LEN - 1)
        after = segment_of(starts_ref, clips, begin + BLOCK_LEN)
        return seg0, seg1, flag(seg0 == seg1).astype(BF16), prior, head, last, after

    def forward(b, carried):
        ur, ui = carried
        seg0, seg1, same, prior, head, last, after = masks(b)
        at = pl.ds(pl.multiple_of(b * BLOCK_LEN, BLOCK_LEN), BLOCK_LEN)
        x = x_ref[at, :]
        xf = x.astype(F32)
        same2 = jnp.concatenate([same, same], axis=1)
        acc = flag(seg0 == prior) * dot(col_p, weigh(ur, ui))
        for j in range(M):
            scaled = jnp.concatenate(
                [(w[2 * j : 2 * j + 1] * xf).astype(BF16), (w[2 * j + 1 : 2 * j + 2] * xf).astype(BF16)], axis=0
            )
            acc = acc + dot(kf[:, j * 256 : j * 256 + 256] * same2, scaled)
        out = skip * xf + acc
        mixed_ref[at, :] = (q_ref[at, :].astype(F32) * out).astype(BF16)
        stack_ref[0, at, :] = (up_ref[at, :].astype(F32) * out).astype(BF16)
        reach = (rows_ref[0, 4 * M : 6 * M, :] * flag(seg1[: 2 * M] == last)).astype(BF16)
        total = dot(reach, x)
        tx[b] = total
        keep = flag(last == prior)
        return (
            total[:M] + keep * (pr * ur - pi * ui),
            total[M:] + keep * (pr * ui + pi * ur),
        )

    lax.fori_loop(0, blocks, forward, (carry_ref[0, :M, :], carry_ref[0, M : 2 * M, :]))
    sums_ref[...] = jnp.zeros_like(sums_ref)

    def backward(step, carried):
        gr, gi = carried
        b = blocks - 1 - step
        seg0, seg1, same, prior, head, last, after = masks(b)
        at = pl.ds(pl.multiple_of(b * BLOCK_LEN, BLOCK_LEN), BLOCK_LEN)
        xf = x_ref[at, :].astype(F32)
        g = up_ref[at, :].astype(F32) * q_ref[at, :].astype(F32)
        gb = g.astype(BF16)
        gx = skip * g + flag(seg0 == after) * dot(col_h, weigh(gr, gi))
        for m in range(2 * M):
            part = dot(kb[m * 128 : m * 128 + 128, :] * same, gb)
            gx = gx + w[m : m + 1] * part
            sums_ref[0, m : m + 1, :] += jnp.sum(xf * part, axis=0, keepdims=True)
        stack_ref[1, at, :] = gx.astype(BF16)
        sums_ref[0, 2 * M : 2 * M + 1, :] += jnp.sum(xf * g, axis=0, keepdims=True)
        total = tx[b]
        join = flag(last == after)
        sums_ref[0, :M, :] += join * (total[:M] * gr - total[M:] * gi)
        sums_ref[0, M : 2 * M, :] -= join * (total[:M] * gi + total[M:] * gr)
        reach = (rows_ref[0, : 2 * M, :] * flag(seg1[: 2 * M] == head)).astype(BF16)
        lead = dot(reach, gb)
        keep = flag(head == after)
        return (
            lead[:M] + keep * (pr * gr - pi * gi),
            lead[M:] + keep * (pr * gi + pi * gr),
        )

    lax.fori_loop(0, blocks, backward, (carry_ref[0, 2 * M : 3 * M, :], carry_ref[0, 3 * M :, :]))


def shards(frames_in, in_proj, log_rates, angles, residues, skip_gain, lengths, grad_out):
    rows = frames_in.shape[1]
    channels = frames_in.shape[2]
    width = in_proj.shape[1]
    M, heads = log_rates.shape
    clips = lengths.shape[1]
    count, mine = lax.axis_size("tm"), lax.axis_index("tm")
    features = lax.all_gather(frames_in, "tensor", axis=2, tiled=True)[0]
    upstream = grad_out[0]
    decay = jnp.exp(log_rates).T
    turn = angles.T
    weight = jnp.sqrt(-jnp.expm1(-2.0 * decay))

    def powers(exponents):
        exponents = jnp.asarray(exponents, F32)
        size = jnp.exp(-decay[:, :, None] * exponents)
        arg = turn[:, :, None] * exponents
        return jnp.concatenate([size * jnp.cos(arg), size * jnp.sin(arg)], axis=1)

    lags = jnp.arange(BLOCK_LEN, dtype=jnp.int32)
    ahead, back, rest = powers(lags), powers(-lags), powers(BLOCK_LEN - lags)
    full = jnp.broadcast_to(powers(jnp.full((1,), BLOCK_LEN)), (heads, 2 * M, BLOCK_LEN))
    row_table = jnp.concatenate([ahead, back, rest, full], axis=1)
    col_table = jnp.concatenate([ahead, back, rest], axis=1).transpose(0, 2, 1)
    span = jnp.arange(rows, dtype=jnp.int32)
    long_table = jnp.concatenate([powers(rows - span), powers(span)], axis=1)
    coeffs = residues.reshape(2, M, heads, 128).transpose(2, 0, 1, 3) * weight[:, None, :, None]
    pad = jnp.zeros((heads, 7, 128), F32)
    w_table = jnp.concatenate(
        [coeffs.reshape(heads, 2 * M, 128), skip_gain.reshape(heads, 1, 128), pad], axis=1
    )
    clip_start = jnp.cumsum(lengths[0]) - lengths[0]
    starts = jnp.concatenate([(mine * rows)[None], clip_start]).astype(jnp.int32)

    pair = 2 if heads % 2 == 0 else 1
    wide = pair * 128
    query_rows, signal, ends = pl.pallas_call(
        functools.partial(project_kernel, clips, M),
        grid_spec=pltpu.PrefetchScalarGridSpec(
            num_scalar_prefetch=1,
            grid=(heads // pair,),
            in_specs=[
                pl.BlockSpec((rows, width), lambda i, s: (0, 0)),
                pl.BlockSpec((2, width, wide), lambda i, s: (0, 0, i)),
                pl.BlockSpec((rows, wide), lambda i, s: (0, i)),
                pl.BlockSpec((pair, 4 * M, rows), lambda i, s: (i, 0, 0)),
            ],
            out_specs=[
                pl.BlockSpec((rows, wide), lambda i, s: (0, i)),
                pl.BlockSpec((rows, wide), lambda i, s: (0, i)),
                pl.BlockSpec((pair, 4 * M, 128), lambda i, s: (i, 0, 0)),
            ],
        ),
        out_shape=[
            jax.ShapeDtypeStruct((rows, channels), BF16),
            jax.ShapeDtypeStruct((rows, channels), BF16),
            jax.ShapeDtypeStruct((heads, 4 * M, 128), F32),
        ],
        compiler_params=pltpu.CompilerParams(vmem_limit_bytes=40 << 20),
        name="project",
    )(starts, features, in_proj, upstream, long_table)

    gathered = lax.all_gather(ends, "tm")
    step = powers(jnp.full((1,), rows))
    step_re, step_im = step[:, :M], step[:, M:]

    def segment_at(frame):
        return jnp.sum((frame >= clip_start).astype(jnp.int32))

    ur = ui = gr = gi = jnp.zeros((heads, M, 128), F32)
    for d in range(count - 1):
        keep = (segment_at(d * rows - 1) == segment_at(d * rows + rows - 1)).astype(F32)
        nr = gathered[d, :, :M] + keep * (step_re * ur - step_im * ui)
        ni = gathered[d, :, M : 2 * M] + keep * (step_re * ui + step_im * ur)
        ur, ui = jnp.where(d < mine, nr, ur), jnp.where(d < mine, ni, ui)
    for d in range(count - 1, 0, -1):
        keep = (segment_at(d * rows) == segment_at(d * rows + rows)).astype(F32)
        nr = gathered[d, :, 2 * M : 3 * M] + keep * (step_re * gr - step_im * gi)
        ni = gathered[d, :, 3 * M :] + keep * (step_re * gi + step_im * gr)
        gr, gi = jnp.where(d > mine, nr, gr), jnp.where(d > mine, ni, gi)
    carries = jnp.concatenate([ur, ui, gr, gi], axis=1)

    per_head = lambda i, s: (i, 0, 0)
    column = lambda i, s: (0, i)
    mixed, stacked, sums = pl.pallas_call(
        functools.partial(conv_kernel, clips, M),
        grid_spec=pltpu.PrefetchScalarGridSpec(
            num_scalar_prefetch=1,
            grid=(heads,),
            in_specs=[
                pl.BlockSpec((1, BLOCK_LEN, 6 * M), per_head),
                pl.BlockSpec((1, 8 * M, BLOCK_LEN), per_head),
                pl.BlockSpec((1, 2 * M + 8, 128), per_head),
                pl.BlockSpec((1, 4 * M, 128), per_head),
                pl.BlockSpec((rows, 128), column),
                pl.BlockSpec((rows, 128), column),
                pl.BlockSpec((rows, 128), column),
            ],
            out_specs=[
                pl.BlockSpec((rows, 128), column),
                pl.BlockSpec((2, rows, 128), lambda i, s: (0, 0, i)),
                pl.BlockSpec((1, 2 * M + 8, 128), per_head),
            ],
            scratch_shapes=[
                pltpu.VMEM((BLOCK_LEN, 2 * M * BLOCK_LEN), BF16),
                pltpu.VMEM((2 * M * BLOCK_LEN, BLOCK_LEN), BF16),
                pltpu.VMEM((rows // BLOCK_LEN, 2 * M, 128), F32),
            ],
        ),
        out_shape=[
            jax.ShapeDtypeStruct((rows, channels), BF16),
            jax.ShapeDtypeStruct((2, rows, channels), BF16),
            jax.ShapeDtypeStruct((heads, 2 * M + 8, 128), F32),
        ],
        compiler_params=pltpu.CompilerParams(vmem_limit_bytes=40 << 20),
        name="conv",
    )(starts, col_table, row_table, w_table, carries, query_rows, signal, upstream)

    norm_scale = 1.0 / math.sqrt(rows * count * lax.axis_size("dp"))
    coeff_term = sums[:, : 2 * M].reshape(heads, 2, M, 128) * (weight[:, None, :, None] * norm_scale)
    coeff_term = coeff_term.transpose(1, 2, 0, 3).reshape(2, M, channels)
    skip_term = sums[:, 2 * M].reshape(channels) * norm_scale
    proj_term = jnp.einsum("ld,klc->kdc", features, stacked, preferred_element_type=F32) * norm_scale
    partial_in = jnp.einsum("klc,kdc->ld", stacked, in_proj, preferred_element_type=F32)
    proj_sum, coeff_sum, skip_sum = lax.psum((proj_term, coeff_term, skip_term), ("tm", "dp"))
    input_grad = lax.psum_scatter(
        partial_in.astype(BF16)[None], "tensor", scatter_dimension=2, tiled=True
    )
    return (mixed[None], input_grad, proj_sum, coeff_sum, skip_sum)


def solution(mesh):
    in_specs = (
        P(("group", "dp"), "tm", "tensor"),
        P(None, None, "tensor"),
        P(None, "tensor"),
        P(None, "tensor"),
        P(None, None, "tensor"),
        P("tensor"),
        P(("group", "dp"), None),
        P(("group", "dp"), "tm", "tensor"),
    )
    out_specs = (
        P(("group", "dp"), "tm", "tensor"),
        P(("group", "dp"), "tm", "tensor"),
        P("group", None, "tensor"),
        P("group", None, "tensor"),
        P(("group", "tensor")),
    )
    return jax.shard_map(shards, mesh=mesh, in_specs=in_specs, out_specs=out_specs, check_vma=False)
```

```python
import functools
import math

import jax
import jax.numpy as jnp
from jax import lax
from jax.experimental import pallas as pl
from jax.experimental.pallas import tpu as pltpu
from jax.sharding import PartitionSpec as P

BLOCK_LEN = 128
F32 = jnp.float32
BF16 = jnp.bfloat16


def dot(a, b):
    return jnp.dot(a, b, preferred_element_type=F32)


def segment_of(starts_ref, clips, frame):
    total = jnp.where(frame >= starts_ref[1], 1, 0)
    for k in range(1, clips):
        total = total + jnp.where(frame >= starts_ref[1 + k], 1, 0)
    return total


def project_kernel(clips, modes, starts_ref, feat_ref, proj_ref, up_ref, table_ref, q_ref, x_ref, ends_ref):
    rows, width = q_ref.shape
    first = starts_ref[0]
    lane = lax.broadcasted_iota(jnp.int32, (1, rows), 1) + first
    seg = segment_of(starts_ref, clips, lane)
    at_end = jnp.where(seg == segment_of(starts_ref, clips, first + rows - 1), 1.0, 0.0)
    at_start = jnp.where(seg == segment_of(starts_ref, clips, first), 1.0, 0.0)
    query = dot(feat_ref[...], proj_ref[0]).astype(BF16)
    q_ref[...] = query
    signal = dot(feat_ref[...], proj_ref[1]).astype(BF16)
    x_ref[...] = signal
    grad = (query.astype(F32) * up_ref[...].astype(F32)).astype(BF16)
    for h in range(width // 128):
        cols = slice(h * 128, h * 128 + 128)
        fwd = (table_ref[h, : 2 * modes, :] * at_end).astype(BF16)
        bwd = (table_ref[h, 2 * modes :, :] * at_start).astype(BF16)
        ends_ref[h, : 2 * modes, :] = dot(fwd, signal[:, cols])
        ends_ref[h, 2 * modes :, :] = dot(bwd, grad[:, cols])


def conv_kernel(
    clips, modes, starts_ref, cols_ref, rows_ref, w_ref, carry_ref, q_ref, x_ref, up_ref,
    mixed_ref, stack_ref, sums_ref, kf, kb, tx,
):
    rows = q_ref.shape[0]
    blocks = rows // BLOCK_LEN
    M = modes
    first = starts_ref[0]
    i0 = lax.broadcasted_iota(jnp.int32, (BLOCK_LEN, BLOCK_LEN), 0)
    i1 = lax.broadcasted_iota(jnp.int32, (BLOCK_LEN, BLOCK_LEN), 1)
    for m in range(M):
        re, im = m, M + m
        er, ei = cols_ref[0, :, re : re + 1], cols_ref[0, :, im : im + 1]
        fr = rows_ref[0, 2 * M + re : 2 * M + re + 1, :]
        fi = rows_ref[0, 2 * M + im : 2 * M + im + 1, :]
        kf[:, re * 128 : re * 128 + 128] = jnp.where(i0 >= i1, er * fr - ei * fi, 0.0).astype(BF16)
        kf[:, im * 128 : im * 128 + 128] = jnp.where(i0 >= i1, -(er * fi + ei * fr), 0.0).astype(BF16)
        fr, fi = cols_ref[0, :, 2 * M + re : 2 * M + re + 1], cols_ref[0, :, 2 * M + im : 2 * M + im + 1]
        er, ei = rows_ref[0, re : re + 1, :], rows_ref[0, im : im + 1, :]
        kb[re * 128 : re * 128 + 128, :] = jnp.where(i1 >= i0, er * fr - ei * fi, 0.0).astype(BF16)
        kb[im * 128 : im * 128 + 128, :] = jnp.where(i1 >= i0, -(er * fi + ei * fr), 0.0).astype(BF16)

    w = w_ref[0, : 2 * M, :]
    wr, wi = w[:M], w[M:]
    skip = w_ref[0, 2 * M : 2 * M + 1, :]
    pr = rows_ref[0, 6 * M : 7 * M, :]
    pi = rows_ref[0, 7 * M : 8 * M, :]
    col_p = cols_ref[0, :, : 2 * M].astype(BF16)
    col_h = cols_ref[0, :, 4 * M : 6 * M].astype(BF16)

    def flag(cond):
        return jnp.where(cond, 1.0, 0.0).astype(F32)

    def weigh(sr, si):
        return jnp.concatenate([wr * sr - wi * si, -(wr * si + wi * sr)], axis=0).astype(BF16)

    def masks(b):
        begin = first + b * BLOCK_LEN
        seg0 = segment_of(starts_ref, clips, i0 + begin)
        seg1 = segment_of(starts_ref, clips, i1 + begin)
        prior = segment_of(starts_ref, clips, begin - 1)
        head = segment_of(starts_ref, clips, begin)
        last = segment_of(starts_ref, clips, begin + BLOCK_LEN - 1)
        after = segment_of(starts_ref, clips, begin + BLOCK_LEN)
        return seg0, seg1, flag(seg0 == seg1).astype(BF16), prior, head, last, after

    def forward(b, carried):
        ur, ui = carried
        seg0, seg1, same, prior, head, last, after = masks(b)
        at = pl.ds(pl.multiple_of(b * BLOCK_LEN, BLOCK_LEN), BLOCK_LEN)
        x = x_ref[at, :]
        xf = x.astype(F32)
        same2 = jnp.concatenate([same, same], axis=1)
        acc = flag(seg0 == prior) * dot(col_p, weigh(ur, ui))
        for j in range(M):
            scaled = jnp.concatenate(
                [(w[2 * j : 2 * j + 1] * xf).astype(BF16), (w[2 * j + 1 : 2 * j + 2] * xf).astype(BF16)], axis=0
            )
            acc = acc + dot(kf[:, j * 256 : j * 256 + 256] * same2, scaled)
        out = skip * xf + acc
        mixed_ref[at, :] = (q_ref[at, :].astype(F32) * out).astype(BF16)
        stack_ref[0, at, :] = (up_ref[at, :].astype(F32) * out).astype(BF16)
        reach = (rows_ref[0, 4 * M : 6 * M, :] * flag(seg1[: 2 * M] == last)).astype(BF16)
        total = dot(reach, x)
        tx[b] = total
        keep = flag(last == prior)
        return (
            total[:M] + keep * (pr * ur - pi * ui),
            total[M:] + keep * (pr * ui + pi * ur),
        )

    lax.fori_loop(0, blocks, forward, (carry_ref[0, :M, :], carry_ref[0, M : 2 * M, :]))
    sums_ref[...] = jnp.zeros_like(sums_ref)

    def backward(step, carried):
        gr, gi = carried
        b = blocks - 1 - step
        seg0, seg1, same, prior, head, last, after = masks(b)
        at = pl.ds(pl.multiple_of(b * BLOCK_LEN, BLOCK_LEN), BLOCK_LEN)
        xf = x_ref[at, :].astype(F32)
        g = up_ref[at, :].astype(F32) * q_ref[at, :].astype(F32)
        gb = g.astype(BF16)
        gx = skip * g + flag(seg0 == after) * dot(col_h, weigh(gr, gi))
        for m in range(2 * M):
            part = dot(kb[m * 128 : m * 128 + 128, :] * same, gb)
            gx = gx + w[m : m + 1] * part
            sums_ref[0, m : m + 1, :] += jnp.sum(xf * part, axis=0, keepdims=True)
        stack_ref[1, at, :] = gx.astype(BF16)
        sums_ref[0, 2 * M : 2 * M + 1, :] += jnp.sum(xf * g, axis=0, keepdims=True)
        total = tx[b]
        join = flag(last == after)
        sums_ref[0, :M, :] += join * (total[:M] * gr - total[M:] * gi)
        sums_ref[0, M : 2 * M, :] -= join * (total[:M] * gi + total[M:] * gr)
        reach = (rows_ref[0, : 2 * M, :] * flag(seg1[: 2 * M] == head)).astype(BF16)
        lead = dot(reach, gb)
        keep = flag(head == after)
        return (
            lead[:M] + keep * (pr * gr - pi * gi),
            lead[M:] + keep * (pr * gi + pi * gr),
        )

    lax.fori_loop(0, blocks, backward, (carry_ref[0, 2 * M : 3 * M, :], carry_ref[0, 3 * M :, :]))


def summed_over(value, axis):
    size = lax.axis_size(axis)
    if size & (size - 1):
        return lax.psum(value, axis)
    stride = 1
    while stride < size:
        value = value + lax.ppermute(value, axis, [(i, i ^ stride) for i in range(size)])
        stride *= 2
    return value


def shards(frames_in, in_proj, log_rates, angles, residues, skip_gain, lengths, grad_out):
    rows = frames_in.shape[1]
    channels = frames_in.shape[2]
    width = in_proj.shape[1]
    M, heads = log_rates.shape
    clips = lengths.shape[1]
    count, mine = lax.axis_size("tm"), lax.axis_index("tm")
    features = lax.all_gather(frames_in, "tensor", axis=2, tiled=True)[0]
    upstream = grad_out[0]
    decay = jnp.exp(log_rates).T
    turn = angles.T
    weight = jnp.sqrt(-jnp.expm1(-2.0 * decay))

    def powers(exponents):
        exponents = jnp.asarray(exponents, F32)
        size = jnp.exp(-decay[:, :, None] * exponents)
        arg = turn[:, :, None] * exponents
        return jnp.concatenate([size * jnp.cos(arg), size * jnp.sin(arg)], axis=1)

    lags = jnp.arange(BLOCK_LEN, dtype=jnp.int32)
    ahead, back, rest = powers(lags), powers(-lags), powers(BLOCK_LEN - lags)
    full = jnp.broadcast_to(powers(jnp.full((1,), BLOCK_LEN)), (heads, 2 * M, BLOCK_LEN))
    row_table = jnp.concatenate([ahead, back, rest, full], axis=1)
    col_table = jnp.concatenate([ahead, back, rest], axis=1).transpose(0, 2, 1)
    span = jnp.arange(rows, dtype=jnp.int32)
    long_table = jnp.concatenate([powers(rows - span), powers(span)], axis=1)
    coeffs = residues.reshape(2, M, heads, 128).transpose(2, 0, 1, 3) * weight[:, None, :, None]
    pad = jnp.zeros((heads, 7, 128), F32)
    w_table = jnp.concatenate(
        [coeffs.reshape(heads, 2 * M, 128), skip_gain.reshape(heads, 1, 128), pad], axis=1
    )
    clip_start = jnp.cumsum(lengths[0]) - lengths[0]
    starts = jnp.concatenate([(mine * rows)[None], clip_start]).astype(jnp.int32)

    pair = 2 if heads % 2 == 0 else 1
    wide = pair * 128
    query_rows, signal, ends = pl.pallas_call(
        functools.partial(project_kernel, clips, M),
        grid_spec=pltpu.PrefetchScalarGridSpec(
            num_scalar_prefetch=1,
            grid=(heads // pair,),
            in_specs=[
                pl.BlockSpec((rows, width), lambda i, s: (0, 0)),
                pl.BlockSpec((2, width, wide), lambda i, s: (0, 0, i)),
                pl.BlockSpec((rows, wide), lambda i, s: (0, i)),
                pl.BlockSpec((pair, 4 * M, rows), lambda i, s: (i, 0, 0)),
            ],
            out_specs=[
                pl.BlockSpec((rows, wide), lambda i, s: (0, i)),
                pl.BlockSpec((rows, wide), lambda i, s: (0, i)),
                pl.BlockSpec((pair, 4 * M, 128), lambda i, s: (i, 0, 0)),
            ],
        ),
        out_shape=[
            jax.ShapeDtypeStruct((rows, channels), BF16),
            jax.ShapeDtypeStruct((rows, channels), BF16),
            jax.ShapeDtypeStruct((heads, 4 * M, 128), F32),
        ],
        compiler_params=pltpu.CompilerParams(vmem_limit_bytes=40 << 20),
        name="project",
    )(starts, features, in_proj, upstream, long_table)

    gathered = lax.all_gather(ends, "tm")
    step = powers(jnp.full((1,), rows))
    step_re, step_im = step[:, :M], step[:, M:]

    def segment_at(frame):
        return jnp.sum((frame >= clip_start).astype(jnp.int32))

    ur = ui = gr = gi = jnp.zeros((heads, M, 128), F32)
    for d in range(count - 1):
        keep = (segment_at(d * rows - 1) == segment_at(d * rows + rows - 1)).astype(F32)
        nr = gathered[d, :, :M] + keep * (step_re * ur - step_im * ui)
        ni = gathered[d, :, M : 2 * M] + keep * (step_re * ui + step_im * ur)
        ur, ui = jnp.where(d < mine, nr, ur), jnp.where(d < mine, ni, ui)
    for d in range(count - 1, 0, -1):
        keep = (segment_at(d * rows) == segment_at(d * rows + rows)).astype(F32)
        nr = gathered[d, :, 2 * M : 3 * M] + keep * (step_re * gr - step_im * gi)
        ni = gathered[d, :, 3 * M :] + keep * (step_re * gi + step_im * gr)
        gr, gi = jnp.where(d > mine, nr, gr), jnp.where(d > mine, ni, gi)
    carries = jnp.concatenate([ur, ui, gr, gi], axis=1)

    per_head = lambda i, s: (i, 0, 0)
    column = lambda i, s: (0, i)
    mixed, stacked, sums = pl.pallas_call(
        functools.partial(conv_kernel, clips, M),
        grid_spec=pltpu.PrefetchScalarGridSpec(
            num_scalar_prefetch=1,
            grid=(heads,),
            in_specs=[
                pl.BlockSpec((1, BLOCK_LEN, 6 * M), per_head),
                pl.BlockSpec((1, 8 * M, BLOCK_LEN), per_head),
                pl.BlockSpec((1, 2 * M + 8, 128), per_head),
                pl.BlockSpec((1, 4 * M, 128), per_head),
                pl.BlockSpec((rows, 128), column),
                pl.BlockSpec((rows, 128), column),
                pl.BlockSpec((rows, 128), column),
            ],
            out_specs=[
                pl.BlockSpec((rows, 128), column),
                pl.BlockSpec((2, rows, 128), lambda i, s: (0, 0, i)),
                pl.BlockSpec((1, 2 * M + 8, 128), per_head),
            ],
            scratch_shapes=[
                pltpu.VMEM((BLOCK_LEN, 2 * M * BLOCK_LEN), BF16),
                pltpu.VMEM((2 * M * BLOCK_LEN, BLOCK_LEN), BF16),
                pltpu.VMEM((rows // BLOCK_LEN, 2 * M, 128), F32),
            ],
        ),
        out_shape=[
            jax.ShapeDtypeStruct((rows, channels), BF16),
            jax.ShapeDtypeStruct((2, rows, channels), BF16),
            jax.ShapeDtypeStruct((heads, 2 * M + 8, 128), F32),
        ],
        compiler_params=pltpu.CompilerParams(vmem_limit_bytes=40 << 20),
        name="conv",
    )(starts, col_table, row_table, w_table, carries, query_rows, signal, upstream)

    norm_scale = 1.0 / math.sqrt(rows * count * lax.axis_size("dp"))
    coeff_term = sums[:, : 2 * M].reshape(heads, 2, M, 128) * (weight[:, None, :, None] * norm_scale)
    coeff_term = coeff_term.transpose(1, 2, 0, 3).reshape(2, M, channels)
    skip_term = sums[:, 2 * M].reshape(channels) * norm_scale
    proj_term = jnp.einsum("ld,klc->kdc", features, stacked, preferred_element_type=F32) * norm_scale
    partial_in = jnp.einsum("klc,kdc->ld", stacked, in_proj, preferred_element_type=F32)
    small = jnp.concatenate([coeff_term.reshape(2 * M, channels), skip_term[None]], axis=0)
    proj_sum = lax.psum(proj_term.astype(BF16), ("tm", "dp")).astype(F32)
    small = summed_over(summed_over(small, "dp"), "tm")
    coeff_sum = small[: 2 * M].reshape(2, M, channels)
    skip_sum = small[2 * M]
    own, size = lax.axis_index("tensor"), lax.axis_size("tensor")
    share = width // size
    total_in = lax.dynamic_slice_in_dim(partial_in, own * share, share, 1)
    for k in range(1, size):
        other = lax.rem(own + k, size)
        piece = lax.dynamic_slice_in_dim(partial_in, other * share, share, 1).astype(BF16)
        total_in += lax.ppermute(piece, "tensor", [(i, (i + k) % size) for i in range(size)]).astype(F32)
    input_grad = total_in.astype(BF16)[None]
    return (mixed[None], input_grad, proj_sum, coeff_sum, skip_sum)


def solution(mesh):
    in_specs = (
        P(("group", "dp"), "tm", "tensor"),
        P(None, None, "tensor"),
        P(None, "tensor"),
        P(None, "tensor"),
        P(None, None, "tensor"),
        P("tensor"),
        P(("group", "dp"), None),
        P(("group", "dp"), "tm", "tensor"),
    )
    out_specs = (
        P(("group", "dp"), "tm", "tensor"),
        P(("group", "dp"), "tm", "tensor"),
        P("group", None, "tensor"),
        P("group", None, "tensor"),
        P(("group", "tensor")),
    )
    return jax.shard_map(shards, mesh=mesh, in_specs=in_specs, out_specs=out_specs, check_vma=False)
```

```python
import functools
import math

import jax
import jax.numpy as jnp
from jax import lax
from jax.experimental import pallas as pl
from jax.experimental.pallas import tpu as pltpu
from jax.sharding import PartitionSpec as P

BLOCK_LEN = 128
F32 = jnp.float32
BF16 = jnp.bfloat16


def dot(a, b):
    return jnp.dot(a, b, preferred_element_type=F32)


def segment_of(starts_ref, clips, frame):
    total = jnp.where(frame >= starts_ref[1], 1, 0)
    for k in range(1, clips):
        total = total + jnp.where(frame >= starts_ref[1 + k], 1, 0)
    return total


def project_kernel(clips, modes, starts_ref, feat_ref, proj_ref, up_ref, tre_ref, tim_ref, q_ref, x_ref, ends_ref):
    rows, width = q_ref.shape
    first = starts_ref[0]
    lane = lax.broadcasted_iota(jnp.int32, (1, rows), 1) + first
    seg = segment_of(starts_ref, clips, lane)
    at_end = jnp.where(seg == segment_of(starts_ref, clips, first + rows - 1), 1.0, 0.0)
    at_start = jnp.where(seg == segment_of(starts_ref, clips, first), 1.0, 0.0)
    query = dot(feat_ref[...], proj_ref[0]).astype(BF16)
    q_ref[...] = query
    signal = dot(feat_ref[...], proj_ref[1]).astype(BF16)
    x_ref[...] = signal
    grad = (query.astype(F32) * up_ref[...].astype(F32)).astype(BF16)
    for h in range(width // 128):
        cols = slice(h * 128, h * 128 + 128)
        fwd = jnp.concatenate([tre_ref[h, :, :rows], tim_ref[h, :, :rows]], axis=0)
        bwd = jnp.concatenate([tre_ref[h, :, rows : 2 * rows], tim_ref[h, :, rows : 2 * rows]], axis=0)
        fwd = (fwd * at_end).astype(BF16)
        bwd = (bwd * at_start).astype(BF16)
        ends_ref[h, : 2 * modes, :] = dot(fwd, signal[:, cols])
        ends_ref[h, 2 * modes :, :] = dot(bwd, grad[:, cols])


def conv_kernel(
    clips, modes, starts_ref, cre_ref, cim_ref, tre_ref, tim_ref, w_ref, u_ref, g_ref, q_ref, x_ref, up_ref,
    mixed_ref, stack_ref, sums_ref, kf, kb, tx,
):
    rows = q_ref.shape[0]
    blocks = rows // BLOCK_LEN
    M = modes
    L = 2 * rows
    first = starts_ref[0]
    i0 = lax.broadcasted_iota(jnp.int32, (BLOCK_LEN, BLOCK_LEN), 0)
    i1 = lax.broadcasted_iota(jnp.int32, (BLOCK_LEN, BLOCK_LEN), 1)
    for m in range(M):
        re, im = m, M + m
        er, ei = cre_ref[0, :128, m : m + 1], cim_ref[0, :128, m : m + 1]
        fr, fi = tre_ref[0, m : m + 1, L + 128 : L + 256], tim_ref[0, m : m + 1, L + 128 : L + 256]
        kf[:, re * 128 : re * 128 + 128] = jnp.where(i0 >= i1, er * fr - ei * fi, 0.0).astype(BF16)
        kf[:, im * 128 : im * 128 + 128] = jnp.where(i0 >= i1, -(er * fi + ei * fr), 0.0).astype(BF16)
        fr, fi = cre_ref[0, 128:256, m : m + 1], cim_ref[0, 128:256, m : m + 1]
        er, ei = tre_ref[0, m : m + 1, L : L + 128], tim_ref[0, m : m + 1, L : L + 128]
        kb[re * 128 : re * 128 + 128, :] = jnp.where(i1 >= i0, er * fr - ei * fi, 0.0).astype(BF16)
        kb[im * 128 : im * 128 + 128, :] = jnp.where(i1 >= i0, -(er * fi + ei * fr), 0.0).astype(BF16)

    w = w_ref[0, : 2 * M, :]
    wr, wi = w[:M], w[M:]
    skip = w_ref[0, 2 * M : 2 * M + 1, :]
    pr = tre_ref[0, :, L + 384 : L + 512]
    pi = tim_ref[0, :, L + 384 : L + 512]
    col_p = jnp.concatenate([cre_ref[0, :128, :], cim_ref[0, :128, :]], axis=1).astype(BF16)
    col_h = jnp.concatenate([cre_ref[0, 256:, :], cim_ref[0, 256:, :]], axis=1).astype(BF16)
    row_h = jnp.concatenate([tre_ref[0, :, L + 256 : L + 384], tim_ref[0, :, L + 256 : L + 384]], axis=0)
    row_p = jnp.concatenate([tre_ref[0, :, L : L + 128], tim_ref[0, :, L : L + 128]], axis=0)

    def flag(cond):
        return jnp.where(cond, 1.0, 0.0).astype(F32)

    def weigh(sr, si):
        return jnp.concatenate([wr * sr - wi * si, -(wr * si + wi * sr)], axis=0).astype(BF16)

    def masks(b):
        begin = first + b * BLOCK_LEN
        seg0 = segment_of(starts_ref, clips, i0 + begin)
        seg1 = segment_of(starts_ref, clips, i1 + begin)
        prior = segment_of(starts_ref, clips, begin - 1)
        head = segment_of(starts_ref, clips, begin)
        last = segment_of(starts_ref, clips, begin + BLOCK_LEN - 1)
        after = segment_of(starts_ref, clips, begin + BLOCK_LEN)
        return seg0, seg1, flag(seg0 == seg1).astype(BF16), prior, head, last, after

    def forward(b, carried):
        ur, ui = carried
        seg0, seg1, same, prior, head, last, after = masks(b)
        at = pl.ds(pl.multiple_of(b * BLOCK_LEN, BLOCK_LEN), BLOCK_LEN)
        x = x_ref[at, :]
        xf = x.astype(F32)
        same2 = jnp.concatenate([same, same], axis=1)
        acc = flag(seg0 == prior) * dot(col_p, weigh(ur, ui))
        for j in range(M):
            scaled = jnp.concatenate(
                [(w[2 * j : 2 * j + 1] * xf).astype(BF16), (w[2 * j + 1 : 2 * j + 2] * xf).astype(BF16)], axis=0
            )
            acc = acc + dot(kf[:, j * 256 : j * 256 + 256] * same2, scaled)
        out = skip * xf + acc
        mixed_ref[at, :] = (q_ref[at, :].astype(F32) * out).astype(BF16)
        stack_ref[0, at, :] = (up_ref[at, :].astype(F32) * out).astype(BF16)
        reach = (row_h * flag(seg1[: 2 * M] == last)).astype(BF16)
        total = dot(reach, x)
        tx[b] = total
        keep = flag(last == prior)
        return (
            total[:M] + keep * (pr * ur - pi * ui),
            total[M:] + keep * (pr * ui + pi * ur),
        )

    lax.fori_loop(0, blocks, forward, (u_ref[0, :M, :], u_ref[0, M:, :]))
    sums_ref[...] = jnp.zeros_like(sums_ref)

    def backward(step, carried):
        gr, gi = carried
        b = blocks - 1 - step
        seg0, seg1, same, prior, head, last, after = masks(b)
        at = pl.ds(pl.multiple_of(b * BLOCK_LEN, BLOCK_LEN), BLOCK_LEN)
        xf = x_ref[at, :].astype(F32)
        g = up_ref[at, :].astype(F32) * q_ref[at, :].astype(F32)
        gb = g.astype(BF16)
        gx = skip * g + flag(seg0 == after) * dot(col_h, weigh(gr, gi))
        for m in range(2 * M):
            part = dot(kb[m * 128 : m * 128 + 128, :] * same, gb)
            gx = gx + w[m : m + 1] * part
            sums_ref[0, m : m + 1, :] += jnp.sum(xf * part, axis=0, keepdims=True)
        stack_ref[1, at, :] = gx.astype(BF16)
        sums_ref[0, 2 * M : 2 * M + 1, :] += jnp.sum(xf * g, axis=0, keepdims=True)
        total = tx[b]
        join = flag(last == after)
        sums_ref[0, :M, :] += join * (total[:M] * gr - total[M:] * gi)
        sums_ref[0, M : 2 * M, :] -= join * (total[:M] * gi + total[M:] * gr)
        reach = (row_p * flag(seg1[: 2 * M] == head)).astype(BF16)
        lead = dot(reach, gb)
        keep = flag(head == after)
        return (
            lead[:M] + keep * (pr * gr - pi * gi),
            lead[M:] + keep * (pr * gi + pi * gr),
        )

    lax.fori_loop(0, blocks, backward, (g_ref[0, :M, :], g_ref[0, M:, :]))


def summed_over(value, axis):
    size = lax.axis_size(axis)
    if size & (size - 1):
        return lax.psum(value, axis)
    stride = 1
    while stride < size:
        value = value + lax.ppermute(value, axis, [(i, i ^ stride) for i in range(size)])
        stride *= 2
    return value


def summed_matrix(value):
    stages = []
    for axis, kind in (("dp", F32), ("tm", BF16)):
        size, place = lax.axis_size(axis), lax.axis_index(axis)
        stride = 1
        while stride < size:
            upper = lax.rem(place // stride, 2)
            pairs = [(i, i ^ stride) for i in range(size)]
            half = value.shape[0] // 2
            away = lax.dynamic_slice_in_dim(value, (1 - upper) * half, half, 0).astype(kind)
            kept = lax.dynamic_slice_in_dim(value, upper * half, half, 0)
            value = kept + lax.ppermute(away, axis, pairs).astype(F32)
            stages.append((axis, pairs, upper))
            stride *= 2
    value = value.astype(BF16)
    for axis, pairs, upper in reversed(stages):
        other = lax.ppermute(value, axis, pairs)
        low, high = jnp.where(upper == 0, value, other), jnp.where(upper == 0, other, value)
        value = jnp.concatenate([low, high], axis=0)
    return value.astype(F32)


def widened(value, axis):
    size, place = lax.axis_size(axis), lax.axis_index(axis)
    pieces = [value]
    for k in range(1, size):
        pieces.append(lax.ppermute(value, axis, [(i, (i + k) % size) for i in range(size)]))
    columns = []
    for j in range(size):
        column = pieces[0]
        for k in range(1, size):
            column = jnp.where(lax.rem(place - j + size, size) == k, pieces[k], column)
        columns.append(column)
    return jnp.concatenate(columns, axis=1)


def shards(frames_in, in_proj, log_rates, angles, residues, skip_gain, lengths, grad_out):
    rows = frames_in.shape[1]
    channels = frames_in.shape[2]
    width = in_proj.shape[1]
    M, heads = log_rates.shape
    clips = lengths.shape[1]
    count, mine = lax.axis_size("tm"), lax.axis_index("tm")
    features = widened(frames_in[0], "tensor")
    upstream = grad_out[0]
    decay = jnp.exp(log_rates).T
    turn = angles.T
    weight = jnp.sqrt(-jnp.expm1(-2.0 * decay))

    lags = jnp.arange(BLOCK_LEN, dtype=jnp.int32)
    span = jnp.arange(rows, dtype=jnp.int32)
    steps = jnp.concatenate(
        [rows - span, span, lags, -lags, BLOCK_LEN - lags, jnp.full_like(lags, BLOCK_LEN)]
    ).astype(F32)
    size = jnp.exp(-decay[:, :, None] * steps)
    table_re = size * jnp.cos(turn[:, :, None] * steps)
    table_im = size * jnp.sin(turn[:, :, None] * steps)
    col_re = table_re[:, :, 2 * rows : 2 * rows + 3 * BLOCK_LEN].transpose(0, 2, 1)
    col_im = table_im[:, :, 2 * rows : 2 * rows + 3 * BLOCK_LEN].transpose(0, 2, 1)
    coeffs = residues.reshape(2, M, heads, 128).transpose(2, 0, 1, 3) * weight[:, None, :, None]
    pad = jnp.zeros((heads, 7, 128), F32)
    w_table = jnp.concatenate(
        [coeffs.reshape(heads, 2 * M, 128), skip_gain.reshape(heads, 1, 128), pad], axis=1
    )
    clip_start = jnp.cumsum(lengths[0]) - lengths[0]
    starts = jnp.concatenate([(mine * rows)[None], clip_start]).astype(jnp.int32)

    pair = 2 if heads % 2 == 0 else 1
    wide = pair * 128
    query_rows, signal, ends = pl.pallas_call(
        functools.partial(project_kernel, clips, M),
        grid_spec=pltpu.PrefetchScalarGridSpec(
            num_scalar_prefetch=1,
            grid=(heads // pair,),
            in_specs=[
                pl.BlockSpec((rows, width), lambda i, s: (0, 0)),
                pl.BlockSpec((2, width, wide), lambda i, s: (0, 0, i)),
                pl.BlockSpec((rows, wide), lambda i, s: (0, i)),
                pl.BlockSpec((pair, M, steps.size), lambda i, s: (i, 0, 0)),
                pl.BlockSpec((pair, M, steps.size), lambda i, s: (i, 0, 0)),
            ],
            out_specs=[
                pl.BlockSpec((rows, wide), lambda i, s: (0, i)),
                pl.BlockSpec((rows, wide), lambda i, s: (0, i)),
                pl.BlockSpec((pair, 4 * M, 128), lambda i, s: (i, 0, 0)),
            ],
        ),
        out_shape=[
            jax.ShapeDtypeStruct((rows, channels), BF16),
            jax.ShapeDtypeStruct((rows, channels), BF16),
            jax.ShapeDtypeStruct((heads, 4 * M, 128), F32),
        ],
        compiler_params=pltpu.CompilerParams(vmem_limit_bytes=40 << 20),
        name="project",
    )(starts, features, in_proj, upstream, table_re, table_im)

    step_re, step_im = table_re[:, :, :1], table_im[:, :, :1]

    def segment_at(frame):
        return jnp.sum((frame >= clip_start).astype(jnp.int32))

    def join(state, own, keep):
        re, im = state[:, :M], state[:, M:]
        turned = jnp.concatenate([step_re * re - step_im * im, step_re * im + step_im * re], axis=1)
        return own + keep.astype(F32) * turned

    entering = leaving = jnp.zeros((heads, 2 * M, 128), F32)
    if count <= 8:
        for k in range(count - 1, 0, -1):
            before = lax.ppermute(ends[:, : 2 * M], "tm", [(i, i + k) for i in range(count - k)])
            behind = lax.ppermute(ends[:, 2 * M :], "tm", [(i + k, i) for i in range(count - k)])
            d = mine - k
            entering = join(
                entering, before, segment_at(d * rows - 1) == segment_at(d * rows + rows - 1)
            )
            d = mine + k
            leaving = join(leaving, behind, segment_at(d * rows) == segment_at(d * rows + rows))
    else:
        gathered = lax.all_gather(ends, "tm")
        for d in range(count - 1):
            keep = segment_at(d * rows - 1) == segment_at(d * rows + rows - 1)
            entering = jnp.where(d < mine, join(entering, gathered[d, :, : 2 * M], keep), entering)
        for d in range(count - 1, 0, -1):
            keep = segment_at(d * rows) == segment_at(d * rows + rows)
            leaving = jnp.where(d > mine, join(leaving, gathered[d, :, 2 * M :], keep), leaving)

    per_head = lambda i, s: (i, 0, 0)
    column = lambda i, s: (0, i)
    mixed, stacked, sums = pl.pallas_call(
        functools.partial(conv_kernel, clips, M),
        grid_spec=pltpu.PrefetchScalarGridSpec(
            num_scalar_prefetch=1,
            grid=(heads,),
            in_specs=[
                pl.BlockSpec((1, 3 * BLOCK_LEN, M), per_head),
                pl.BlockSpec((1, 3 * BLOCK_LEN, M), per_head),
                pl.BlockSpec((1, M, steps.size), per_head),
                pl.BlockSpec((1, M, steps.size), per_head),
                pl.BlockSpec((1, 2 * M + 8, 128), per_head),
                pl.BlockSpec((1, 2 * M, 128), per_head),
                pl.BlockSpec((1, 2 * M, 128), per_head),
                pl.BlockSpec((rows, 128), column),
                pl.BlockSpec((rows, 128), column),
                pl.BlockSpec((rows, 128), column),
            ],
            out_specs=[
                pl.BlockSpec((rows, 128), column),
                pl.BlockSpec((2, rows, 128), lambda i, s: (0, 0, i)),
                pl.BlockSpec((1, 2 * M + 8, 128), per_head),
            ],
            scratch_shapes=[
                pltpu.VMEM((BLOCK_LEN, 2 * M * BLOCK_LEN), BF16),
                pltpu.VMEM((2 * M * BLOCK_LEN, BLOCK_LEN), BF16),
                pltpu.VMEM((rows // BLOCK_LEN, 2 * M, 128), F32),
            ],
        ),
        out_shape=[
            jax.ShapeDtypeStruct((rows, channels), BF16),
            jax.ShapeDtypeStruct((2, rows, channels), BF16),
            jax.ShapeDtypeStruct((heads, 2 * M + 8, 128), F32),
        ],
        compiler_params=pltpu.CompilerParams(vmem_limit_bytes=40 << 20),
        name="conv",
    )(starts, col_re, col_im, table_re, table_im, w_table, entering, leaving, query_rows, signal, upstream)

    norm_scale = 1.0 / math.sqrt(rows * count * lax.axis_size("dp"))
    coeff_term = sums[:, : 2 * M].reshape(heads, 2, M, 128) * (weight[:, None, :, None] * norm_scale)
    coeff_term = coeff_term.transpose(1, 2, 0, 3).reshape(2, M, channels)
    skip_term = sums[:, 2 * M].reshape(channels) * norm_scale
    proj_terms = [
        jnp.einsum("ld,lc->dc", features, stacked[k], preferred_element_type=F32) * norm_scale
        for k in range(2)
    ]
    partial_in = jnp.einsum("klc,kdc->ld", stacked, in_proj, preferred_element_type=F32)
    small = jnp.concatenate([coeff_term.reshape(2 * M, channels), skip_term[None]], axis=0)
    proj_sum = jnp.stack([summed_matrix(term) for term in proj_terms])
    small = summed_over(summed_over(small, "dp"), "tm")
    coeff_sum = small[: 2 * M].reshape(2, M, channels)
    skip_sum = small[2 * M]
    own, size = lax.axis_index("tensor"), lax.axis_size("tensor")
    share = width // size
    total_in = lax.dynamic_slice_in_dim(partial_in, own * share, share, 1)
    for k in range(1, size):
        other = lax.rem(own + k, size)
        piece = lax.dynamic_slice_in_dim(partial_in, other * share, share, 1).astype(BF16)
        total_in += lax.ppermute(piece, "tensor", [(i, (i + k) % size) for i in range(size)]).astype(F32)
    input_grad = total_in.astype(BF16)[None]
    return (mixed[None], input_grad, proj_sum, coeff_sum, skip_sum)


def solution(mesh):
    in_specs = (
        P(("group", "dp"), "tm", "tensor"),
        P(None, None, "tensor"),
        P(None, "tensor"),
        P(None, "tensor"),
        P(None, None, "tensor"),
        P("tensor"),
        P(("group", "dp"), None),
        P(("group", "dp"), "tm", "tensor"),
    )
    out_specs = (
        P(("group", "dp"), "tm", "tensor"),
        P(("group", "dp"), "tm", "tensor"),
        P("group", None, "tensor"),
        P("group", None, "tensor"),
        P(("group", "tensor")),
    )
    return jax.shard_map(shards, mesh=mesh, in_specs=in_specs, out_specs=out_specs, check_vma=False)
```

```python
import functools
import math

import jax
import jax.numpy as jnp
from jax import lax
from jax.experimental import pallas as pl
from jax.experimental.pallas import tpu as pltpu
from jax.sharding import PartitionSpec as P

BLOCK_LEN = 128
F32 = jnp.float32
BF16 = jnp.bfloat16


def dot(a, b):
    return jnp.dot(a, b, preferred_element_type=F32)


def segment_of(starts_ref, clips, frame):
    total = jnp.where(frame >= starts_ref[1], 1, 0)
    for k in range(1, clips):
        total = total + jnp.where(frame >= starts_ref[1 + k], 1, 0)
    return total


def project_kernel(clips, modes, starts_ref, feat_ref, proj_ref, up_ref, tre_ref, tim_ref, q_ref, x_ref, ends_ref):
    rows, width = q_ref.shape
    first = starts_ref[0]
    lane = lax.broadcasted_iota(jnp.int32, (1, rows), 1) + first
    seg = segment_of(starts_ref, clips, lane)
    at_end = jnp.where(seg == segment_of(starts_ref, clips, first + rows - 1), 1.0, 0.0)
    at_start = jnp.where(seg == segment_of(starts_ref, clips, first), 1.0, 0.0)
    query = dot(feat_ref[...], proj_ref[0]).astype(BF16)
    q_ref[...] = query
    signal = dot(feat_ref[...], proj_ref[1]).astype(BF16)
    x_ref[...] = signal
    grad = (query.astype(F32) * up_ref[...].astype(F32)).astype(BF16)
    for h in range(width // 128):
        cols = slice(h * 128, h * 128 + 128)
        fwd = jnp.concatenate([tre_ref[h, :, :rows], tim_ref[h, :, :rows]], axis=0)
        bwd = jnp.concatenate([tre_ref[h, :, rows : 2 * rows], tim_ref[h, :, rows : 2 * rows]], axis=0)
        fwd = (fwd * at_end).astype(BF16)
        bwd = (bwd * at_start).astype(BF16)
        ends_ref[h, : 2 * modes, :] = dot(fwd, signal[:, cols])
        ends_ref[h, 2 * modes :, :] = dot(bwd, grad[:, cols])


def conv_kernel(
    clips, modes, starts_ref, cre_ref, cim_ref, tre_ref, tim_ref, w_ref, u_ref, g_ref, q_ref, x_ref, up_ref,
    mixed_ref, stack_ref, sums_ref, kf, kb, tx,
):
    rows = q_ref.shape[0]
    blocks = rows // BLOCK_LEN
    M = modes
    L = 2 * rows
    first = starts_ref[0]
    i0 = lax.broadcasted_iota(jnp.int32, (BLOCK_LEN, BLOCK_LEN), 0)
    i1 = lax.broadcasted_iota(jnp.int32, (BLOCK_LEN, BLOCK_LEN), 1)
    for m in range(M):
        re, im = m, M + m
        er, ei = cre_ref[0, :128, m : m + 1], cim_ref[0, :128, m : m + 1]
        fr, fi = tre_ref[0, m : m + 1, L + 128 : L + 256], tim_ref[0, m : m + 1, L + 128 : L + 256]
        kf[:, re * 128 : re * 128 + 128] = jnp.where(i0 >= i1, er * fr - ei * fi, 0.0).astype(BF16)
        kf[:, im * 128 : im * 128 + 128] = jnp.where(i0 >= i1, -(er * fi + ei * fr), 0.0).astype(BF16)
        fr, fi = cre_ref[0, 128:256, m : m + 1], cim_ref[0, 128:256, m : m + 1]
        er, ei = tre_ref[0, m : m + 1, L : L + 128], tim_ref[0, m : m + 1, L : L + 128]
        kb[re * 128 : re * 128 + 128, :] = jnp.where(i1 >= i0, er * fr - ei * fi, 0.0).astype(BF16)
        kb[im * 128 : im * 128 + 128, :] = jnp.where(i1 >= i0, -(er * fi + ei * fr), 0.0).astype(BF16)

    w = w_ref[0, : 2 * M, :]
    wr, wi = w[:M], w[M:]
    skip = w_ref[0, 2 * M : 2 * M + 1, :]
    pr = tre_ref[0, :, L + 384 : L + 512]
    pi = tim_ref[0, :, L + 384 : L + 512]
    col_p = jnp.concatenate([cre_ref[0, :128, :], cim_ref[0, :128, :]], axis=1).astype(BF16)
    col_h = jnp.concatenate([cre_ref[0, 256:, :], cim_ref[0, 256:, :]], axis=1).astype(BF16)
    row_h = jnp.concatenate([tre_ref[0, :, L + 256 : L + 384], tim_ref[0, :, L + 256 : L + 384]], axis=0)
    row_p = jnp.concatenate([tre_ref[0, :, L : L + 128], tim_ref[0, :, L : L + 128]], axis=0)

    def flag(cond):
        return jnp.where(cond, 1.0, 0.0).astype(F32)

    def weigh(sr, si):
        return jnp.concatenate([wr * sr - wi * si, -(wr * si + wi * sr)], axis=0).astype(BF16)

    def masks(b):
        begin = first + b * BLOCK_LEN
        seg0 = segment_of(starts_ref, clips, i0 + begin)
        seg1 = segment_of(starts_ref, clips, i1 + begin)
        prior = segment_of(starts_ref, clips, begin - 1)
        head = segment_of(starts_ref, clips, begin)
        last = segment_of(starts_ref, clips, begin + BLOCK_LEN - 1)
        after = segment_of(starts_ref, clips, begin + BLOCK_LEN)
        return seg0, seg1, flag(seg0 == seg1).astype(BF16), prior, head, last, after

    def forward(b, carried):
        ur, ui = carried
        seg0, seg1, same, prior, head, last, after = masks(b)
        at = pl.ds(pl.multiple_of(b * BLOCK_LEN, BLOCK_LEN), BLOCK_LEN)
        x = x_ref[at, :]
        xf = x.astype(F32)
        same2 = jnp.concatenate([same, same], axis=1)
        acc = flag(seg0 == prior) * dot(col_p, weigh(ur, ui))
        for j in range(M):
            scaled = jnp.concatenate(
                [(w[2 * j : 2 * j + 1] * xf).astype(BF16), (w[2 * j + 1 : 2 * j + 2] * xf).astype(BF16)], axis=0
            )
            acc = acc + dot(kf[:, j * 256 : j * 256 + 256] * same2, scaled)
        out = skip * xf + acc
        mixed_ref[at, :] = (q_ref[at, :].astype(F32) * out).astype(BF16)
        stack_ref[0, at, :] = (up_ref[at, :].astype(F32) * out).astype(BF16)
        reach = (row_h * flag(seg1[: 2 * M] == last)).astype(BF16)
        total = dot(reach, x)
        tx[b] = total
        keep = flag(last == prior)
        return (
            total[:M] + keep * (pr * ur - pi * ui),
            total[M:] + keep * (pr * ui + pi * ur),
        )

    lax.fori_loop(0, blocks, forward, (u_ref[0, :M, :], u_ref[0, M:, :]))
    sums_ref[...] = jnp.zeros_like(sums_ref)

    def backward(step, carried):
        gr, gi = carried
        b = blocks - 1 - step
        seg0, seg1, same, prior, head, last, after = masks(b)
        at = pl.ds(pl.multiple_of(b * BLOCK_LEN, BLOCK_LEN), BLOCK_LEN)
        xf = x_ref[at, :].astype(F32)
        g = up_ref[at, :].astype(F32) * q_ref[at, :].astype(F32)
        gb = g.astype(BF16)
        gx = skip * g + flag(seg0 == after) * dot(col_h, weigh(gr, gi))
        for m in range(2 * M):
            part = dot(kb[m * 128 : m * 128 + 128, :] * same, gb)
            gx = gx + w[m : m + 1] * part
            sums_ref[0, m : m + 1, :] += jnp.sum(xf * part, axis=0, keepdims=True)
        stack_ref[1, at, :] = gx.astype(BF16)
        sums_ref[0, 2 * M : 2 * M + 1, :] += jnp.sum(xf * g, axis=0, keepdims=True)
        total = tx[b]
        join = flag(last == after)
        sums_ref[0, :M, :] += join * (total[:M] * gr - total[M:] * gi)
        sums_ref[0, M : 2 * M, :] -= join * (total[:M] * gi + total[M:] * gr)
        reach = (row_p * flag(seg1[: 2 * M] == head)).astype(BF16)
        lead = dot(reach, gb)
        keep = flag(head == after)
        return (
            lead[:M] + keep * (pr * gr - pi * gi),
            lead[M:] + keep * (pr * gi + pi * gr),
        )

    lax.fori_loop(0, blocks, backward, (g_ref[0, :M, :], g_ref[0, M:, :]))


def summed_over(value, axis):
    size = lax.axis_size(axis)
    if size & (size - 1):
        return lax.psum(value, axis)
    stride = 1
    while stride < size:
        value = value + lax.ppermute(value, axis, [(i, i ^ stride) for i in range(size)])
        stride *= 2
    return value


def summed_matrix(value):
    stages = []
    for axis, kind in (("dp", F32), ("tm", BF16)):
        size, place = lax.axis_size(axis), lax.axis_index(axis)
        stride = 1
        while stride < size:
            upper = lax.rem(place // stride, 2)
            pairs = [(i, i ^ stride) for i in range(size)]
            half = value.shape[0] // 2
            away = lax.dynamic_slice_in_dim(value, (1 - upper) * half, half, 0).astype(kind)
            kept = lax.dynamic_slice_in_dim(value, upper * half, half, 0)
            value = kept + lax.ppermute(away, axis, pairs).astype(F32)
            stages.append((axis, pairs, upper))
            stride *= 2
    value = value.astype(BF16)
    for axis, pairs, upper in reversed(stages):
        other = lax.ppermute(value, axis, pairs)
        low, high = jnp.where(upper == 0, value, other), jnp.where(upper == 0, other, value)
        value = jnp.concatenate([low, high], axis=0)
    return value.astype(F32)


def widened(value, axis):
    size, place = lax.axis_size(axis), lax.axis_index(axis)
    pieces = [value]
    for k in range(1, size):
        pieces.append(lax.ppermute(value, axis, [(i, (i + k) % size) for i in range(size)]))
    columns = []
    for j in range(size):
        column = pieces[0]
        for k in range(1, size):
            column = jnp.where(lax.rem(place - j + size, size) == k, pieces[k], column)
        columns.append(column)
    return jnp.concatenate(columns, axis=1)


def shards(frames_in, in_proj, log_rates, angles, residues, skip_gain, lengths, grad_out):
    rows = frames_in.shape[1]
    channels = frames_in.shape[2]
    width = in_proj.shape[1]
    M, heads = log_rates.shape
    clips = lengths.shape[1]
    count, mine = lax.axis_size("tm"), lax.axis_index("tm")
    features = widened(frames_in[0], "tensor")
    upstream = grad_out[0]
    decay = jnp.exp(log_rates).T
    turn = angles.T
    weight = jnp.sqrt(-jnp.expm1(-2.0 * decay))

    lags = jnp.arange(BLOCK_LEN, dtype=jnp.int32)
    span = jnp.arange(rows, dtype=jnp.int32)
    steps = jnp.concatenate(
        [rows - span, span, lags, -lags, BLOCK_LEN - lags, jnp.full_like(lags, BLOCK_LEN)]
    ).astype(F32)
    size = jnp.exp(-decay[:, :, None] * steps)
    table_re = size * jnp.cos(turn[:, :, None] * steps)
    table_im = size * jnp.sin(turn[:, :, None] * steps)
    col_re = table_re[:, :, 2 * rows : 2 * rows + 3 * BLOCK_LEN].transpose(0, 2, 1)
    col_im = table_im[:, :, 2 * rows : 2 * rows + 3 * BLOCK_LEN].transpose(0, 2, 1)
    coeffs = residues.reshape(2, M, heads, 128).transpose(2, 0, 1, 3) * weight[:, None, :, None]
    pad = jnp.zeros((heads, 7, 128), F32)
    w_table = jnp.concatenate(
        [coeffs.reshape(heads, 2 * M, 128), skip_gain.reshape(heads, 1, 128), pad], axis=1
    )
    clip_start = jnp.cumsum(lengths[0]) - lengths[0]
    starts = jnp.concatenate([(mine * rows)[None], clip_start]).astype(jnp.int32)

    pair = 2 if heads % 2 == 0 else 1
    wide = pair * 128
    query_rows, signal, ends = pl.pallas_call(
        functools.partial(project_kernel, clips, M),
        grid_spec=pltpu.PrefetchScalarGridSpec(
            num_scalar_prefetch=1,
            grid=(heads // pair,),
            in_specs=[
                pl.BlockSpec((rows, width), lambda i, s: (0, 0)),
                pl.BlockSpec((2, width, wide), lambda i, s: (0, 0, i)),
                pl.BlockSpec((rows, wide), lambda i, s: (0, i)),
                pl.BlockSpec((pair, M, steps.size), lambda i, s: (i, 0, 0)),
                pl.BlockSpec((pair, M, steps.size), lambda i, s: (i, 0, 0)),
            ],
            out_specs=[
                pl.BlockSpec((rows, wide), lambda i, s: (0, i)),
                pl.BlockSpec((rows, wide), lambda i, s: (0, i)),
                pl.BlockSpec((pair, 4 * M, 128), lambda i, s: (i, 0, 0)),
            ],
        ),
        out_shape=[
            jax.ShapeDtypeStruct((rows, channels), BF16),
            jax.ShapeDtypeStruct((rows, channels), BF16),
            jax.ShapeDtypeStruct((heads, 4 * M, 128), F32),
        ],
        compiler_params=pltpu.CompilerParams(vmem_limit_bytes=40 << 20),
        name="project",
    )(starts, features, in_proj, upstream, table_re, table_im)

    step_re, step_im = table_re[:, :, :1], table_im[:, :, :1]

    def segment_at(frame):
        return jnp.sum((frame >= clip_start).astype(jnp.int32))

    def join(state, own, keep):
        re, im = state[:, :M], state[:, M:]
        turned = jnp.concatenate([step_re * re - step_im * im, step_re * im + step_im * re], axis=1)
        return own + keep.astype(F32) * turned

    entering = leaving = jnp.zeros((heads, 2 * M, 128), F32)
    gathered = lax.all_gather(ends, "tm")
    for d in range(count - 1):
        keep = segment_at(d * rows - 1) == segment_at(d * rows + rows - 1)
        entering = jnp.where(d < mine, join(entering, gathered[d, :, : 2 * M], keep), entering)
    for d in range(count - 1, 0, -1):
        keep = segment_at(d * rows) == segment_at(d * rows + rows)
        leaving = jnp.where(d > mine, join(leaving, gathered[d, :, 2 * M :], keep), leaving)

    per_head = lambda i, s: (i, 0, 0)
    column = lambda i, s: (0, i)
    mixed, stacked, sums = pl.pallas_call(
        functools.partial(conv_kernel, clips, M),
        grid_spec=pltpu.PrefetchScalarGridSpec(
            num_scalar_prefetch=1,
            grid=(heads,),
            in_specs=[
                pl.BlockSpec((1, 3 * BLOCK_LEN, M), per_head),
                pl.BlockSpec((1, 3 * BLOCK_LEN, M), per_head),
                pl.BlockSpec((1, M, steps.size), per_head),
                pl.BlockSpec((1, M, steps.size), per_head),
                pl.BlockSpec((1, 2 * M + 8, 128), per_head),
                pl.BlockSpec((1, 2 * M, 128), per_head),
                pl.BlockSpec((1, 2 * M, 128), per_head),
                pl.BlockSpec((rows, 128), column),
                pl.BlockSpec((rows, 128), column),
                pl.BlockSpec((rows, 128), column),
            ],
            out_specs=[
                pl.BlockSpec((rows, 128), column),
                pl.BlockSpec((2, rows, 128), lambda i, s: (0, 0, i)),
                pl.BlockSpec((1, 2 * M + 8, 128), per_head),
            ],
            scratch_shapes=[
                pltpu.VMEM((BLOCK_LEN, 2 * M * BLOCK_LEN), BF16),
                pltpu.VMEM((2 * M * BLOCK_LEN, BLOCK_LEN), BF16),
                pltpu.VMEM((rows // BLOCK_LEN, 2 * M, 128), F32),
            ],
        ),
        out_shape=[
            jax.ShapeDtypeStruct((rows, channels), BF16),
            jax.ShapeDtypeStruct((2, rows, channels), BF16),
            jax.ShapeDtypeStruct((heads, 2 * M + 8, 128), F32),
        ],
        compiler_params=pltpu.CompilerParams(vmem_limit_bytes=40 << 20),
        name="conv",
    )(starts, col_re, col_im, table_re, table_im, w_table, entering, leaving, query_rows, signal, upstream)

    norm_scale = 1.0 / math.sqrt(rows * count * lax.axis_size("dp"))
    coeff_term = sums[:, : 2 * M].reshape(heads, 2, M, 128) * (weight[:, None, :, None] * norm_scale)
    coeff_term = coeff_term.transpose(1, 2, 0, 3).reshape(2, M, channels)
    skip_term = sums[:, 2 * M].reshape(channels) * norm_scale
    proj_terms = [
        jnp.einsum("ld,lc->dc", features, stacked[k], preferred_element_type=F32) * norm_scale
        for k in range(2)
    ]
    partial_in = jnp.einsum("klc,kdc->ld", stacked, in_proj, preferred_element_type=F32)
    small = jnp.concatenate([coeff_term.reshape(2 * M, channels), skip_term[None]], axis=0)
    proj_sum = jnp.stack([summed_matrix(term) for term in proj_terms])
    small = summed_over(summed_over(small, "dp"), "tm")
    coeff_sum = small[: 2 * M].reshape(2, M, channels)
    skip_sum = small[2 * M]
    own, size = lax.axis_index("tensor"), lax.axis_size("tensor")
    share = width // size
    total_in = lax.dynamic_slice_in_dim(partial_in, own * share, share, 1)
    for k in range(1, size):
        other = lax.rem(own + k, size)
        piece = lax.dynamic_slice_in_dim(partial_in, other * share, share, 1).astype(BF16)
        total_in += lax.ppermute(piece, "tensor", [(i, (i + k) % size) for i in range(size)]).astype(F32)
    input_grad = total_in.astype(BF16)[None]
    return (mixed[None], input_grad, proj_sum, coeff_sum, skip_sum)


def solution(mesh):
    in_specs = (
        P(("group", "dp"), "tm", "tensor"),
        P(None, None, "tensor"),
        P(None, "tensor"),
        P(None, "tensor"),
        P(None, None, "tensor"),
        P("tensor"),
        P(("group", "dp"), None),
        P(("group", "dp"), "tm", "tensor"),
    )
    out_specs = (
        P(("group", "dp"), "tm", "tensor"),
        P(("group", "dp"), "tm", "tensor"),
        P("group", None, "tensor"),
        P("group", None, "tensor"),
        P(("group", "tensor")),
    )
    return jax.shard_map(shards, mesh=mesh, in_specs=in_specs, out_specs=out_specs, check_vma=False)
```

```python
import functools
import math

import jax
import jax.numpy as jnp
from jax import lax
from jax.experimental import pallas as pl
from jax.experimental.pallas import tpu as pltpu
from jax.sharding import PartitionSpec as P

BLOCK_LEN = 128
F32 = jnp.float32
BF16 = jnp.bfloat16


def dot(a, b):
    return jnp.dot(a, b, preferred_element_type=F32)


def segment_of(starts_ref, clips, frame):
    total = jnp.where(frame >= starts_ref[1], 1, 0)
    for k in range(1, clips):
        total = total + jnp.where(frame >= starts_ref[1 + k], 1, 0)
    return total


def project_kernel(clips, modes, starts_ref, feat_ref, proj_ref, up_ref, tre_ref, tim_ref, q_ref, x_ref, ends_ref):
    rows, width = q_ref.shape
    first = starts_ref[0]
    lane = lax.broadcasted_iota(jnp.int32, (1, rows), 1) + first
    seg = segment_of(starts_ref, clips, lane)
    at_end = jnp.where(seg == segment_of(starts_ref, clips, first + rows - 1), 1.0, 0.0)
    at_start = jnp.where(seg == segment_of(starts_ref, clips, first), 1.0, 0.0)
    query = dot(feat_ref[...], proj_ref[0]).astype(BF16)
    q_ref[...] = query
    signal = dot(feat_ref[...], proj_ref[1]).astype(BF16)
    x_ref[...] = signal
    grad = (query.astype(F32) * up_ref[...].astype(F32)).astype(BF16)
    for h in range(width // 128):
        cols = slice(h * 128, h * 128 + 128)
        fwd = jnp.concatenate([tre_ref[h, :, :rows], tim_ref[h, :, :rows]], axis=0)
        bwd = jnp.concatenate([tre_ref[h, :, rows : 2 * rows], tim_ref[h, :, rows : 2 * rows]], axis=0)
        fwd = (fwd * at_end).astype(BF16)
        bwd = (bwd * at_start).astype(BF16)
        ends_ref[h, : 2 * modes, :] = dot(fwd, signal[:, cols])
        ends_ref[h, 2 * modes :, :] = dot(bwd, grad[:, cols])


def forward_kernel(
    clips, modes, starts_ref, cre_ref, cim_ref, tre_ref, tim_ref, w_ref, u_ref, q_ref, x_ref, up_ref,
    mixed_ref, grad_ref, tx, kf,
):
    rows = q_ref.shape[0]
    blocks = rows // BLOCK_LEN
    M = modes
    L = 2 * rows
    first = starts_ref[0]
    i0 = lax.broadcasted_iota(jnp.int32, (BLOCK_LEN, BLOCK_LEN), 0)
    i1 = lax.broadcasted_iota(jnp.int32, (BLOCK_LEN, BLOCK_LEN), 1)
    for m in range(M):
        re, im = m, M + m
        er, ei = cre_ref[0, :128, m : m + 1], cim_ref[0, :128, m : m + 1]
        fr, fi = tre_ref[0, m : m + 1, L + 128 : L + 256], tim_ref[0, m : m + 1, L + 128 : L + 256]
        kf[:, re * 128 : re * 128 + 128] = jnp.where(i0 >= i1, er * fr - ei * fi, 0.0).astype(BF16)
        kf[:, im * 128 : im * 128 + 128] = jnp.where(i0 >= i1, -(er * fi + ei * fr), 0.0).astype(BF16)

    w = w_ref[0, : 2 * M, :]
    wr, wi = w[:M], w[M:]
    skip = w_ref[0, 2 * M : 2 * M + 1, :]
    pr = tre_ref[0, :, L + 384 : L + 512]
    pi = tim_ref[0, :, L + 384 : L + 512]
    col_p = jnp.concatenate([cre_ref[0, :128, :], cim_ref[0, :128, :]], axis=1).astype(BF16)
    col_h = jnp.concatenate([cre_ref[0, 256:, :], cim_ref[0, 256:, :]], axis=1).astype(BF16)
    row_h = jnp.concatenate([tre_ref[0, :, L + 256 : L + 384], tim_ref[0, :, L + 256 : L + 384]], axis=0)
    row_p = jnp.concatenate([tre_ref[0, :, L : L + 128], tim_ref[0, :, L : L + 128]], axis=0)

    def flag(cond):
        return jnp.where(cond, 1.0, 0.0).astype(F32)

    def weigh(sr, si):
        return jnp.concatenate([wr * sr - wi * si, -(wr * si + wi * sr)], axis=0).astype(BF16)

    def masks(b):
        begin = first + b * BLOCK_LEN
        seg0 = segment_of(starts_ref, clips, i0 + begin)
        seg1 = segment_of(starts_ref, clips, i1 + begin)
        prior = segment_of(starts_ref, clips, begin - 1)
        head = segment_of(starts_ref, clips, begin)
        last = segment_of(starts_ref, clips, begin + BLOCK_LEN - 1)
        after = segment_of(starts_ref, clips, begin + BLOCK_LEN)
        return seg0, seg1, flag(seg0 == seg1).astype(BF16), prior, head, last, after

    def forward(b, carried):
        ur, ui = carried
        seg0, seg1, same, prior, head, last, after = masks(b)
        at = pl.ds(pl.multiple_of(b * BLOCK_LEN, BLOCK_LEN), BLOCK_LEN)
        x = x_ref[at, :]
        xf = x.astype(F32)
        same2 = jnp.concatenate([same, same], axis=1)
        acc = flag(seg0 == prior) * dot(col_p, weigh(ur, ui))
        for j in range(M):
            scaled = jnp.concatenate(
                [(w[2 * j : 2 * j + 1] * xf).astype(BF16), (w[2 * j + 1 : 2 * j + 2] * xf).astype(BF16)], axis=0
            )
            acc = acc + dot(kf[:, j * 256 : j * 256 + 256] * same2, scaled)
        out = skip * xf + acc
        mixed_ref[at, :] = (q_ref[at, :].astype(F32) * out).astype(BF16)
        grad_ref[at, :] = (up_ref[at, :].astype(F32) * out).astype(BF16)
        reach = (row_h * flag(seg1[: 2 * M] == last)).astype(BF16)
        total = dot(reach, x)
        tx[0, b] = total
        keep = flag(last == prior)
        return (
            total[:M] + keep * (pr * ur - pi * ui),
            total[M:] + keep * (pr * ui + pi * ur),
        )

    lax.fori_loop(0, blocks, forward, (u_ref[0, :M, :], u_ref[0, M:, :]))


def backward_kernel(
    clips, modes, starts_ref, cre_ref, cim_ref, tre_ref, tim_ref, w_ref, g_ref, q_ref, x_ref, up_ref, tx,
    grad_ref, sums_ref, kb,
):
    rows = q_ref.shape[0]
    blocks = rows // BLOCK_LEN
    M = modes
    L = 2 * rows
    first = starts_ref[0]
    i0 = lax.broadcasted_iota(jnp.int32, (BLOCK_LEN, BLOCK_LEN), 0)
    i1 = lax.broadcasted_iota(jnp.int32, (BLOCK_LEN, BLOCK_LEN), 1)
    for m in range(M):
        re, im = m, M + m
        fr, fi = cre_ref[0, 128:256, m : m + 1], cim_ref[0, 128:256, m : m + 1]
        er, ei = tre_ref[0, m : m + 1, L : L + 128], tim_ref[0, m : m + 1, L : L + 128]
        kb[re * 128 : re * 128 + 128, :] = jnp.where(i1 >= i0, er * fr - ei * fi, 0.0).astype(BF16)
        kb[im * 128 : im * 128 + 128, :] = jnp.where(i1 >= i0, -(er * fi + ei * fr), 0.0).astype(BF16)

    w = w_ref[0, : 2 * M, :]
    wr, wi = w[:M], w[M:]
    skip = w_ref[0, 2 * M : 2 * M + 1, :]
    pr = tre_ref[0, :, L + 384 : L + 512]
    pi = tim_ref[0, :, L + 384 : L + 512]
    col_p = jnp.concatenate([cre_ref[0, :128, :], cim_ref[0, :128, :]], axis=1).astype(BF16)
    col_h = jnp.concatenate([cre_ref[0, 256:, :], cim_ref[0, 256:, :]], axis=1).astype(BF16)
    row_h = jnp.concatenate([tre_ref[0, :, L + 256 : L + 384], tim_ref[0, :, L + 256 : L + 384]], axis=0)
    row_p = jnp.concatenate([tre_ref[0, :, L : L + 128], tim_ref[0, :, L : L + 128]], axis=0)

    def flag(cond):
        return jnp.where(cond, 1.0, 0.0).astype(F32)

    def weigh(sr, si):
        return jnp.concatenate([wr * sr - wi * si, -(wr * si + wi * sr)], axis=0).astype(BF16)

    def masks(b):
        begin = first + b * BLOCK_LEN
        seg0 = segment_of(starts_ref, clips, i0 + begin)
        seg1 = segment_of(starts_ref, clips, i1 + begin)
        prior = segment_of(starts_ref, clips, begin - 1)
        head = segment_of(starts_ref, clips, begin)
        last = segment_of(starts_ref, clips, begin + BLOCK_LEN - 1)
        after = segment_of(starts_ref, clips, begin + BLOCK_LEN)
        return seg0, seg1, flag(seg0 == seg1).astype(BF16), prior, head, last, after

    sums_ref[...] = jnp.zeros_like(sums_ref)

    def backward(step, carried):
        gr, gi = carried
        b = blocks - 1 - step
        seg0, seg1, same, prior, head, last, after = masks(b)
        at = pl.ds(pl.multiple_of(b * BLOCK_LEN, BLOCK_LEN), BLOCK_LEN)
        xf = x_ref[at, :].astype(F32)
        g = up_ref[at, :].astype(F32) * q_ref[at, :].astype(F32)
        gb = g.astype(BF16)
        gx = skip * g + flag(seg0 == after) * dot(col_h, weigh(gr, gi))
        for m in range(2 * M):
            part = dot(kb[m * 128 : m * 128 + 128, :] * same, gb)
            gx = gx + w[m : m + 1] * part
            sums_ref[0, m : m + 1, :] += jnp.sum(xf * part, axis=0, keepdims=True)
        grad_ref[at, :] = gx.astype(BF16)
        sums_ref[0, 2 * M : 2 * M + 1, :] += jnp.sum(xf * g, axis=0, keepdims=True)
        total = tx[0, b]
        join = flag(last == after)
        sums_ref[0, :M, :] += join * (total[:M] * gr - total[M:] * gi)
        sums_ref[0, M : 2 * M, :] -= join * (total[:M] * gi + total[M:] * gr)
        reach = (row_p * flag(seg1[: 2 * M] == head)).astype(BF16)
        lead = dot(reach, gb)
        keep = flag(head == after)
        return (
            lead[:M] + keep * (pr * gr - pi * gi),
            lead[M:] + keep * (pr * gi + pi * gr),
        )

    lax.fori_loop(0, blocks, backward, (g_ref[0, :M, :], g_ref[0, M:, :]))


def summed_over(value, axis):
    size = lax.axis_size(axis)
    if size & (size - 1):
        return lax.psum(value, axis)
    stride = 1
    while stride < size:
        value = value + lax.ppermute(value, axis, [(i, i ^ stride) for i in range(size)])
        stride *= 2
    return value


def halved(value, axes, stages):
    for axis, kind in axes:
        size, place = lax.axis_size(axis), lax.axis_index(axis)
        stride = 1
        while stride < size:
            upper = lax.rem(place // stride, 2)
            pairs = [(i, i ^ stride) for i in range(size)]
            half = value.shape[0] // 2
            away = lax.dynamic_slice_in_dim(value, (1 - upper) * half, half, 0).astype(kind)
            kept = lax.dynamic_slice_in_dim(value, upper * half, half, 0)
            value = kept + lax.ppermute(away, axis, pairs).astype(F32)
            stages.append((axis, pairs, upper))
            stride *= 2
    return value


def doubled(value, stages):
    value = value.astype(BF16)
    for axis, pairs, upper in reversed(stages):
        other = lax.ppermute(value, axis, pairs)
        low, high = jnp.where(upper == 0, value, other), jnp.where(upper == 0, other, value)
        value = jnp.concatenate([low, high], axis=0)
    return value.astype(F32)


def widened(value, axis):
    size, place = lax.axis_size(axis), lax.axis_index(axis)
    pieces = [value]
    for k in range(1, size):
        pieces.append(lax.ppermute(value, axis, [(i, (i + k) % size) for i in range(size)]))
    columns = []
    for j in range(size):
        column = pieces[0]
        for k in range(1, size):
            column = jnp.where(lax.rem(place - j + size, size) == k, pieces[k], column)
        columns.append(column)
    return jnp.concatenate(columns, axis=1)


def shards(frames_in, in_proj, log_rates, angles, residues, skip_gain, lengths, grad_out):
    rows = frames_in.shape[1]
    channels = frames_in.shape[2]
    width = in_proj.shape[1]
    M, heads = log_rates.shape
    clips = lengths.shape[1]
    count, mine = lax.axis_size("tm"), lax.axis_index("tm")
    features = widened(frames_in[0], "tensor")
    upstream = grad_out[0]
    decay = jnp.exp(log_rates).T
    turn = angles.T
    weight = jnp.sqrt(-jnp.expm1(-2.0 * decay))

    lags = jnp.arange(BLOCK_LEN, dtype=jnp.int32)
    span = jnp.arange(rows, dtype=jnp.int32)
    steps = jnp.concatenate(
        [rows - span, span, lags, -lags, BLOCK_LEN - lags, jnp.full_like(lags, BLOCK_LEN)]
    ).astype(F32)
    size = jnp.exp(-decay[:, :, None] * steps)
    table_re = size * jnp.cos(turn[:, :, None] * steps)
    table_im = size * jnp.sin(turn[:, :, None] * steps)
    col_re = table_re[:, :, 2 * rows : 2 * rows + 3 * BLOCK_LEN].transpose(0, 2, 1)
    col_im = table_im[:, :, 2 * rows : 2 * rows + 3 * BLOCK_LEN].transpose(0, 2, 1)
    coeffs = residues.reshape(2, M, heads, 128).transpose(2, 0, 1, 3) * weight[:, None, :, None]
    pad = jnp.zeros((heads, 7, 128), F32)
    w_table = jnp.concatenate(
        [coeffs.reshape(heads, 2 * M, 128), skip_gain.reshape(heads, 1, 128), pad], axis=1
    )
    clip_start = jnp.cumsum(lengths[0]) - lengths[0]
    starts = jnp.concatenate([(mine * rows)[None], clip_start]).astype(jnp.int32)

    pair = 2 if heads % 2 == 0 else 1
    wide = pair * 128
    query_rows, signal, ends = pl.pallas_call(
        functools.partial(project_kernel, clips, M),
        grid_spec=pltpu.PrefetchScalarGridSpec(
            num_scalar_prefetch=1,
            grid=(heads // pair,),
            in_specs=[
                pl.BlockSpec((rows, width), lambda i, s: (0, 0)),
                pl.BlockSpec((2, width, wide), lambda i, s: (0, 0, i)),
                pl.BlockSpec((rows, wide), lambda i, s: (0, i)),
                pl.BlockSpec((pair, M, steps.size), lambda i, s: (i, 0, 0)),
                pl.BlockSpec((pair, M, steps.size), lambda i, s: (i, 0, 0)),
            ],
            out_specs=[
                pl.BlockSpec((rows, wide), lambda i, s: (0, i)),
                pl.BlockSpec((rows, wide), lambda i, s: (0, i)),
                pl.BlockSpec((pair, 4 * M, 128), lambda i, s: (i, 0, 0)),
            ],
        ),
        out_shape=[
            jax.ShapeDtypeStruct((rows, channels), BF16),
            jax.ShapeDtypeStruct((rows, channels), BF16),
            jax.ShapeDtypeStruct((heads, 4 * M, 128), F32),
        ],
        compiler_params=pltpu.CompilerParams(vmem_limit_bytes=40 << 20),
        name="project",
    )(starts, features, in_proj, upstream, table_re, table_im)

    step_re, step_im = table_re[:, :, :1], table_im[:, :, :1]

    def segment_at(frame):
        return jnp.sum((frame >= clip_start).astype(jnp.int32))

    def join(state, own, keep):
        re, im = state[:, :M], state[:, M:]
        turned = jnp.concatenate([step_re * re - step_im * im, step_re * im + step_im * re], axis=1)
        return own + keep.astype(F32) * turned

    entering = leaving = jnp.zeros((heads, 2 * M, 128), F32)
    gathered = lax.all_gather(ends, "tm")
    for d in range(count - 1):
        keep = segment_at(d * rows - 1) == segment_at(d * rows + rows - 1)
        entering = jnp.where(d < mine, join(entering, gathered[d, :, : 2 * M], keep), entering)
    for d in range(count - 1, 0, -1):
        keep = segment_at(d * rows) == segment_at(d * rows + rows)
        leaving = jnp.where(d > mine, join(leaving, gathered[d, :, 2 * M :], keep), leaving)

    per_head = lambda i, s: (i, 0, 0)
    column = lambda i, s: (0, i)
    blocks = rows // BLOCK_LEN
    shared = [
        pl.BlockSpec((1, 3 * BLOCK_LEN, M), per_head),
        pl.BlockSpec((1, 3 * BLOCK_LEN, M), per_head),
        pl.BlockSpec((1, M, steps.size), per_head),
        pl.BlockSpec((1, M, steps.size), per_head),
        pl.BlockSpec((1, 2 * M + 8, 128), per_head),
        pl.BlockSpec((1, 2 * M, 128), per_head),
        pl.BlockSpec((rows, 128), column),
        pl.BlockSpec((rows, 128), column),
        pl.BlockSpec((rows, 128), column),
    ]
    totals_spec = pl.BlockSpec((1, blocks, 2 * M, 128), lambda i, s: (i, 0, 0, 0))
    cost = pl.CostEstimate(
        flops=4 * M * BLOCK_LEN * rows * channels * 4, bytes_accessed=10 * rows * channels, transcendentals=0
    )
    mixed, grad_query, totals = pl.pallas_call(
        functools.partial(forward_kernel, clips, M),
        grid_spec=pltpu.PrefetchScalarGridSpec(
            num_scalar_prefetch=1,
            grid=(heads,),
            in_specs=shared,
            out_specs=[pl.BlockSpec((rows, 128), column), pl.BlockSpec((rows, 128), column), totals_spec],
            scratch_shapes=[pltpu.VMEM((BLOCK_LEN, 2 * M * BLOCK_LEN), BF16)],
        ),
        out_shape=[
            jax.ShapeDtypeStruct((rows, channels), BF16),
            jax.ShapeDtypeStruct((rows, channels), BF16),
            jax.ShapeDtypeStruct((heads, blocks, 2 * M, 128), F32),
        ],
        compiler_params=pltpu.CompilerParams(vmem_limit_bytes=40 << 20),
        cost_estimate=cost,
        name="conv_forward",
    )(starts, col_re, col_im, table_re, table_im, w_table, entering, query_rows, signal, upstream)
    norm_scale = 1.0 / math.sqrt(rows * count * lax.axis_size("dp"))
    query_stages, value_stages = [], []
    query_term = jnp.einsum("ld,lc->dc", features, grad_query, preferred_element_type=F32) * norm_scale
    query_term = halved(query_term, [("dp", F32), ("tm", BF16)], query_stages)
    grad_value, sums = pl.pallas_call(
        functools.partial(backward_kernel, clips, M),
        grid_spec=pltpu.PrefetchScalarGridSpec(
            num_scalar_prefetch=1,
            grid=(heads,),
            in_specs=shared + [totals_spec],
            out_specs=[pl.BlockSpec((rows, 128), column), pl.BlockSpec((1, 2 * M + 8, 128), per_head)],
            scratch_shapes=[pltpu.VMEM((2 * M * BLOCK_LEN, BLOCK_LEN), BF16)],
        ),
        out_shape=[
            jax.ShapeDtypeStruct((rows, channels), BF16),
            jax.ShapeDtypeStruct((heads, 2 * M + 8, 128), F32),
        ],
        compiler_params=pltpu.CompilerParams(vmem_limit_bytes=40 << 20),
        cost_estimate=cost,
        name="conv_backward",
    )(starts, col_re, col_im, table_re, table_im, w_table, leaving, query_rows, signal, upstream, totals)

    coeff_term = sums[:, : 2 * M].reshape(heads, 2, M, 128) * (weight[:, None, :, None] * norm_scale)
    coeff_term = coeff_term.transpose(1, 2, 0, 3).reshape(2, M, channels)
    skip_term = sums[:, 2 * M].reshape(channels) * norm_scale
    value_term = jnp.einsum("ld,lc->dc", features, grad_value, preferred_element_type=F32) * norm_scale
    query_term, value_term = lax.optimization_barrier((query_term, value_term))
    value_term = halved(value_term, [("dp", F32), ("tm", BF16)], value_stages)
    partial_in = jnp.einsum("lc,dc->ld", grad_query, in_proj[0], preferred_element_type=F32)
    partial_in += jnp.einsum("lc,dc->ld", grad_value, in_proj[1], preferred_element_type=F32)
    small = jnp.concatenate([coeff_term.reshape(2 * M, channels), skip_term[None]], axis=0)
    proj_sum = jnp.stack([doubled(query_term, query_stages), doubled(value_term, value_stages)])
    small = summed_over(summed_over(small, "dp"), "tm")
    coeff_sum = small[: 2 * M].reshape(2, M, channels)
    skip_sum = small[2 * M]
    own, size = lax.axis_index("tensor"), lax.axis_size("tensor")
    share = width // size
    total_in = lax.dynamic_slice_in_dim(partial_in, own * share, share, 1)
    for k in range(1, size):
        other = lax.rem(own + k, size)
        piece = lax.dynamic_slice_in_dim(partial_in, other * share, share, 1).astype(BF16)
        total_in += lax.ppermute(piece, "tensor", [(i, (i + k) % size) for i in range(size)]).astype(F32)
    input_grad = total_in.astype(BF16)[None]
    return (mixed[None], input_grad, proj_sum, coeff_sum, skip_sum)


def solution(mesh):
    in_specs = (
        P(("group", "dp"), "tm", "tensor"),
        P(None, None, "tensor"),
        P(None, "tensor"),
        P(None, "tensor"),
        P(None, None, "tensor"),
        P("tensor"),
        P(("group", "dp"), None),
        P(("group", "dp"), "tm", "tensor"),
    )
    out_specs = (
        P(("group", "dp"), "tm", "tensor"),
        P(("group", "dp"), "tm", "tensor"),
        P("group", None, "tensor"),
        P("group", None, "tensor"),
        P(("group", "tensor")),
    )
    return jax.shard_map(shards, mesh=mesh, in_specs=in_specs, out_specs=out_specs, check_vma=False)
```
